128 devices in a mesh: ctx: 32 (over y, x, core), head: 4 (over z).
Axes of the slice: x: 4, y: 4, z: 4, core: 2. Of those that a mesh axis runs over, the one named last changes fastest.
Arguments:
- queries: bfloat16 [4096, 4096], P('ctx', 'head'), may hold values from -6 to 6
- key_input: bfloat16 [2, 4096, 4096], P(None, 'ctx', 'head'), may hold values from -6 to 6
- value_input: bfloat16 [2, 4096, 4096], P(None, 'ctx', 'head'), may hold values from -6 to 6
- beta_rates: float32 [32, 2, 4096], P('head', None, 'ctx'), may hold values from 0 to 1.9, as said below
- out_grad: bfloat16 [4096, 4096], P(('ctx', 'head')), may hold values from -0.75 to 0.75
- out_weight: bfloat16 [4096, 4096], P('head'), may hold values from -0.09375 to 0.09375
Outputs:
- grad_queries: bfloat16 [4096, 4096], P('ctx', 'head')
- grad_keys: bfloat16 [2, 4096, 4096], P(None, 'ctx', 'head')
- grad_values: bfloat16 [2, 4096, 4096], P(None, 'ctx', 'head')
- grad_rates: float32 [32, 2, 4096], P('head', None, 'ctx')
The draws below stay inside these ranges and needn't reach their ends.
Inputs may be any that keep to these rules, and one draw needn't show every extreme that they name: `beta_rates`: positive strengths.
All inputs are finite; a program needn't handle non-finite values.
Results may differ from the reference program's by a relative error of at most 0.011.
Values may be sent and summed in bfloat16 or wider, within the bound.
No kernel may reach another device: no remote copies, remote signals or barrier semaphores. Data moves between devices by JAX's collectives and lax.ppermute only.
A program may use at most 192 MiB of HBM per device.

```python
import jax
import jax.numpy as jnp
from jax import lax

D = 4096
HEADS = 32
HEAD_DIM = 128
HOUSE = 2
BLOCK = 64
TOKENS = 4096


def draw_beta_rates(key, part):
    pick_key, slow_key, fast_key, jitter_key = jax.random.split(key, 4)
    slow_share = 0.5
    slow_heads = jax.random.uniform(pick_key, (HEADS, 1, 1)) < slow_share
    base_rate = HEAD_DIM / (HOUSE * TOKENS)
    slow_rate = base_rate * jnp.exp(jax.random.uniform(slow_key, (HEADS, 1, 1), minval=jnp.log(0.05), maxval=0.0))
    fast_rate = jnp.exp(jax.random.uniform(fast_key, (HEADS, 1, 1), minval=jnp.log(0.3), maxval=jnp.log(1.5)))
    jitter = jnp.exp(jax.random.uniform(jitter_key, (HEADS, HOUSE, TOKENS), minval=-0.7, maxval=0.7))
    rates = jnp.where(slow_heads, slow_rate, fast_rate) * jitter
    return jnp.clip(rates, 1e-06, 1.9).astype(jnp.float32)


def levels(rng, shape, cuts, low, top_value):
    gain = 1.0
    for dim, blocks in cuts:
        draws = jax.random.uniform(jax.random.fold_in(jax.random.fold_in(rng, 6), dim), (blocks,), jnp.float32, low / len(cuts), top_value / len(cuts))
        gain = gain * jnp.repeat(jnp.exp(draws), shape[dim] // blocks).reshape((-1,) + (1,) * (len(shape) - 1 - dim))
    return gain


def centred(rng, extent, spread, bound, cuts=(), held_as=jnp.bfloat16):
    result = spread * jax.random.normal(rng, extent, jnp.float32)
    if cuts:
        result = result * levels(rng, extent, cuts, -0.22, 0.18)
    return jnp.clip(result, -bound, bound).astype(held_as)


def setup_inputs(seed: int = 0) -> dict:
    streams_of = jax.random.split(jax.random.key(seed), 7)
    return {
        "queries": centred(streams_of[0], (TOKENS, HEADS * HEAD_DIM), 1.0, 6.0, ((0, 32), (1, 4))),
        "key_input": centred(streams_of[1], (HOUSE, TOKENS, HEADS * HEAD_DIM), 1.0, 6.0, ((1, 32), (2, 4))),
        "value_input": centred(streams_of[2], (HOUSE, TOKENS, HEADS * HEAD_DIM), 1.0, 6.0, ((1, 32), (2, 4))),
        "beta_rates": draw_beta_rates(jax.random.fold_in(streams_of[6], 71), 0),
        "out_grad": centred(streams_of[4], (TOKENS, D), 0.05, 0.75, ((0, 128),)),
        "out_weight": centred(streams_of[5], (HEADS * HEAD_DIM, D), (HEADS * HEAD_DIM) ** -0.5, 0.09375, ((0, 4),)),
    }


highest = lax.Precision.HIGHEST

def block_solve(key_rows, value_rows, rate_rows):
    length = key_rows.shape[1]
    gram = jnp.einsum('bik,bjk->bij', key_rows, key_rows, precision=highest)
    strict = jnp.tril(jnp.ones((length, length), key_rows.dtype), -1)
    system = jnp.eye(length, dtype=key_rows.dtype) + gram * rate_rows[:, None, :] * strict
    joined = jnp.concatenate([key_rows, value_rows], axis=2)
    solved = jax.scipy.linalg.solve_triangular(system, joined, lower=True, unit_diagonal=True)
    return (solved[..., :key_rows.shape[2]], solved[..., key_rows.shape[2]:])

def read_mask(query_rows, length, dtype):
    house_count = length // query_rows
    upper = house_count * (jnp.arange(query_rows) + 1)
    return (jnp.arange(length)[None, :] < upper[:, None]).astype(dtype)

def block_step(state_in, pieces):
    query_rows, key_rows, value_rows, rate_rows = pieces
    solved_k, solved_v = block_solve(key_rows, value_rows, rate_rows)
    errors = jnp.einsum('bik,bkv->biv', solved_k, state_in, precision=highest) - solved_v
    weighted = errors * rate_rows[:, :, None]
    scores = jnp.einsum('btk,bik->bti', query_rows, key_rows, precision=highest)
    scores = scores * read_mask(query_rows.shape[1], key_rows.shape[1], scores.dtype)[None]
    outputs = jnp.einsum('btk,bkv->btv', query_rows, state_in, precision=highest)
    outputs = outputs - jnp.einsum('bti,biv->btv', scores, weighted, precision=highest)
    state_out = state_in - jnp.einsum('bik,biv->bkv', key_rows, weighted, precision=highest)
    return (state_out, outputs)

def arrange(query_all, raw_keys, value_all, rate_all, block_len):
    tokens, head_count, head_width = query_all.shape
    house_count = raw_keys.shape[0]
    scaling = lax.rsqrt(lax.optimization_barrier(jnp.sum(raw_keys * raw_keys, axis=-1, keepdims=True)) + 1e-06)
    normed = raw_keys * scaling
    blocks = tokens // block_len
    query_blocks = query_all.reshape(blocks, block_len, head_count, head_width).transpose(0, 2, 1, 3)

    def reorder(tensor):
        last_width = tensor.shape[-1]
        shaped = tensor.reshape(house_count, blocks, block_len, head_count, last_width)
        return shaped.transpose(1, 3, 2, 0, 4).reshape(blocks, head_count, block_len * house_count, last_width)
    rate_blocks = rate_all.reshape(head_count, house_count, blocks, block_len)
    rate_blocks = rate_blocks.transpose(2, 0, 3, 1).reshape(blocks, head_count, block_len * house_count)
    return (query_blocks, reorder(normed), reorder(value_all), rate_blocks)

def run_blocks(state_in, query_all, raw_keys, value_all, rate_all, block_len):
    tokens, head_count, head_width = query_all.shape
    pieces = arrange(query_all * head_width ** (-0.5), raw_keys, value_all, rate_all, block_len)
    final, outputs_all = lax.scan(jax.checkpoint(block_step), state_in, pieces)
    return (outputs_all.transpose(0, 2, 1, 3).reshape(tokens, head_count, -1), final)

def reference(queries, key_input, value_input, beta_rates, out_grad, out_weight):
    d_attn = lax.dot_general(out_grad.astype(jnp.float32), out_weight.astype(jnp.float32), (((1,), (1,)), ((), ())), preferred_element_type=jnp.float32).astype(jnp.bfloat16)
    tokens = queries.shape[0]
    query_all = queries.astype(jnp.float32).reshape(tokens, HEADS, HEAD_DIM)
    raw_keys = key_input.astype(jnp.float32).reshape(HOUSE, tokens, HEADS, HEAD_DIM)
    value_all = value_input.astype(jnp.float32).reshape(HOUSE, tokens, HEADS, HEAD_DIM)
    start = jnp.zeros((HEADS, HEAD_DIM, HEAD_DIM), jnp.float32)

    def forward(query_arg, key_arg, value_arg, rate_arg):
        return run_blocks(start, query_arg, key_arg, value_arg, rate_arg, BLOCK)[0]
    outputs_all, pullback = jax.vjp(forward, query_all, raw_keys, value_all, beta_rates)
    grad_q, grad_k, grad_v, grad_b = pullback(d_attn.astype(jnp.float32).reshape(tokens, HEADS, HEAD_DIM))
    return (grad_q.reshape(tokens, HEADS * HEAD_DIM).astype(jnp.bfloat16), grad_k.reshape(HOUSE, tokens, HEADS * HEAD_DIM).astype(jnp.bfloat16), grad_v.reshape(HOUSE, tokens, HEADS * HEAD_DIM).astype(jnp.bfloat16), grad_b)
```

```python
import functools

import jax
import jax.numpy as jnp
from jax import lax
from jax.experimental import pallas as pl
from jax.experimental.pallas import tpu as pltpu
from jax.sharding import PartitionSpec as P

WIDTH = 128
HALF = 4
PER_STEP = 2
SCALE = WIDTH ** (-0.5)
bf16 = jnp.bfloat16
f32 = jnp.float32


def dims(left, right):
    return (((left,), (right,)), ((), ()))


def nn(a, b):
    return lax.dot_general(a, b, dims(1, 0), preferred_element_type=f32)


def nt(a, b):
    return lax.dot_general(a, b, dims(1, 1), preferred_element_type=f32)


def tn(a, b):
    return lax.dot_general(a, b, dims(0, 0), preferred_element_type=f32)


def split(x):
    high = x.astype(bf16)
    return high, (x - high.astype(f32)).astype(bf16)


def iota(shape, dim):
    return lax.broadcasted_iota(jnp.int32, shape, dim)


def order(shape, dim):
    index = iota(shape, dim)
    tokens = shape[dim] // 2
    return jnp.where(index < tokens, 2 * index, 2 * (index - tokens) + 1)


def level_table(rows):
    left = order((rows, rows), 0)
    right = order((rows, rows), 1)
    differ = left ^ right
    level = jnp.zeros((rows, rows), jnp.int32)
    for bit in range(1, (rows - 1).bit_length()):
        level = level + (differ >= (1 << bit)).astype(jnp.int32)
    return jnp.where(left > right, level, -1)


def eye_mask(rows):
    return iota((rows, rows), 0) == iota((rows, rows), 1)


def column(row, diagonal):
    return jnp.sum(jnp.where(diagonal, row, 0.0), axis=1, keepdims=True)


def inverse_norms(keys):
    wide = keys.astype(f32)
    return lax.rsqrt(jnp.sum(wide * wide, axis=1, keepdims=True) + 1e-06)


def pick(ref, head):
    lanes = slice(head * WIDTH, (head + 1) * WIDTH)
    return jnp.concatenate([ref[0, :, lanes], ref[1, :, lanes]], axis=0)


def rate_row(ref, head):
    return jnp.concatenate([ref[head, 0:1, :], ref[head, 1:2, :]], axis=1)


def maps_kernel(place, k_ref, v_ref, b_ref, send_ref, keep_ref, nh_ref, nl_ref, y_ref, z_ref, level_ref):
    step = pl.program_id(0)
    rows = level_ref.shape[0]

    @pl.when(step == 0)
    def _():
        level_ref[...] = level_table(rows)

    diagonal = eye_mask(rows)
    heads = range(PER_STEP)
    keys = [pick(k_ref, h) for h in heads]
    values = [pick(v_ref, h) for h in heads]
    rates = [rate_row(b_ref, h) for h in heads]
    rate_cols = [column(r, diagonal) for r in rates]
    norms = [inverse_norms(k) for k in keys]
    grams = []
    for h in heads:
        raw = nt(keys[h], keys[h])
        norm_row = lax.rsqrt(jnp.sum(jnp.where(diagonal, raw, 0.0), axis=0, keepdims=True) + 1e-06)
        grams.append(jnp.where(level_ref[...] >= 0, raw * norms[h] * norm_row, 0.0))
    systems = [grams[h] * rates[h] for h in heads]
    ident = jnp.where(diagonal, 1.0, 0.0).astype(f32)
    inverse = [ident - jnp.where(level_ref[...] == 0, systems[h], 0.0) for h in heads]
    for level in range(1, (rows - 1).bit_length()):
        rounded = [t.astype(bf16) for t in inverse]
        inner = [
            nn(jnp.where(level_ref[...] == level, systems[h], 0.0).astype(bf16), rounded[h]).astype(bf16)
            for h in heads
        ]
        inverse = [inverse[h] - nn(rounded[h], inner[h]) for h in heads]
    rounded = [t.astype(bf16) for t in inverse]
    core_high = [nn(rounded[h], grams[h].astype(bf16)).astype(bf16) for h in heads]
    residual = []
    for h in heads:
        high, low = split(systems[h])
        residual.append(grams[h] - core_high[h].astype(f32) - nn(high, core_high[h]) - nn(low, core_high[h]))
    core_low = [nn(rounded[h], residual[h].astype(bf16)).astype(bf16) for h in heads]
    for h in heads:
        nh_ref[h] = core_high[h]
        nl_ref[h] = core_low[h]
    for h in heads:
        both = jnp.concatenate([keys[h].astype(f32) * norms[h], values[h].astype(f32)], axis=1)
        high, low = split(both * rate_cols[h])
        solved = both - nn(core_high[h], high) - nn(core_low[h], high) - nn(core_high[h], low)
        y_ref[h] = solved[:, :WIDTH]
        z_ref[h] = solved[:, WIDTH:]
        high, low = split(solved * (rate_cols[h] * norms[h]))
        mapped = (tn(keys[h], high) + tn(keys[h], low)).astype(bf16)
        steps_half = HALF // PER_STEP

        @pl.when(step < steps_half)
        def _():
            send_ref[step * PER_STEP + h] = mapped

        @pl.when(step >= steps_half)
        def _():
            keep_ref[(step - steps_half) * PER_STEP + h] = mapped


def local_grad_kernel(place, og_ref, w_ref, k_ref, q_ref, b_ref, y_ref, send_ref, keep_ref, do_ref, u_ref):
    step = pl.program_id(0)
    steps_half = HALF // PER_STEP
    tokens = q_ref.shape[0]
    rows = 2 * tokens
    diagonal = eye_mask(rows)
    seen = order((rows, tokens), 0) < 2 * (iota((rows, tokens), 1) + 1)
    for h in range(PER_STEP):
        lanes = slice(h * WIDTH, (h + 1) * WIDTH)
        grad = nt(og_ref[...], w_ref[lanes, :]).astype(bf16)
        do_ref[h] = grad
        keys = pick(k_ref, h)
        query = q_ref[:, lanes]
        rate_col = column(rate_row(b_ref, h), diagonal)
        scores = jnp.where(seen, nt(keys, query) * (inverse_norms(keys) * SCALE), 0.0)
        high, low = split(scores)
        reached = nn(high, grad) + nn(low, grad)
        u_ref[h] = reached
        uh, ul = split(reached * rate_col)
        yh, yl = split(y_ref[h])
        local = (tn(query, grad) * SCALE - tn(yh, uh) - tn(yl, uh) - tn(yh, ul)).astype(bf16)

        @pl.when(step < steps_half)
        def _():
            send_ref[step * PER_STEP + h] = local

        @pl.when(step >= steps_half)
        def _():
            keep_ref[(step - steps_half) * PER_STEP + h] = local


def pair_kernel(place, keep_ref, got_ref, gkeep_ref, ggot_ref, *outs):
    core = place[0]
    spot = place[1]
    for shift in range(HALF):
        slot = lax.rem(spot + shift, HALF)
        mine, other = keep_ref[slot].astype(f32), got_ref[slot].astype(f32)
        first = jnp.where(core == 0, mine, other)
        second = jnp.where(core == 0, other, mine)
        mine, other = gkeep_ref[slot].astype(f32), ggot_ref[slot].astype(f32)
        gfirst = jnp.where(core == 0, mine, other)
        gsecond = jnp.where(core == 0, other, mine)
        joined = first + second - nn(second[:, :WIDTH].astype(bf16), first.astype(bf16))
        gjoined = gfirst + gsecond - tn(first[:, :WIDTH].astype(bf16), gsecond.astype(bf16))
        outs[shift][:, : 2 * WIDTH] = joined.astype(bf16)
        outs[shift][:, 2 * WIDTH :] = gjoined.astype(bf16)


def join(first, second):
    forward = first[:, : 2 * WIDTH] + second[:, : 2 * WIDTH]
    forward = forward - nn(second[:, :WIDTH].astype(bf16), first[:, : 2 * WIDTH].astype(bf16))
    backward = first[:, 2 * WIDTH :] + second[:, 2 * WIDTH :]
    backward = backward - tn(first[:, :WIDTH].astype(bf16), second[:, 2 * WIDTH :].astype(bf16))
    return jnp.concatenate([forward, backward], axis=1)


def gather_slots(slots, refs, spot):
    for shift in range(HALF):
        slots[lax.rem(spot + HALF - shift, HALF)] = refs[shift][...]


def row_kernel(place, a_ref, b_ref, c_ref, d_ref, out_ref, slots):
    gather_slots(slots, (a_ref, b_ref, c_ref, d_ref), place[1])
    maps = [slots[i].astype(f32) for i in range(HALF)]
    out_ref[...] = join(join(maps[0], maps[1]), join(maps[2], maps[3])).astype(bf16)


def advance(block, state):
    high, low = split(state)
    moved = nn(block[:, :WIDTH], jnp.concatenate([high, low], axis=1))
    return state - moved[:, :WIDTH] - moved[:, WIDTH:] + block[:, WIDTH : 2 * WIDTH].astype(f32)


def retreat(block, grad):
    high, low = split(grad)
    moved = tn(block[:, :WIDTH], jnp.concatenate([high, low], axis=1))
    return grad - moved[:, :WIDTH] - moved[:, WIDTH:] + block[:, 2 * WIDTH :].astype(f32)


def expand_kernel(place, a_ref, b_ref, c_ref, d_ref, e_ref, f_ref, g_ref, h_ref, o0, o1, o2, o3, chips, lines, found):
    spot, line = place[1], place[2]
    gather_slots(chips, (a_ref, b_ref, c_ref, d_ref), spot)
    gather_slots(lines, (e_ref, f_ref, g_ref, h_ref), line)
    state = jnp.zeros((WIDTH, WIDTH), f32)
    grad = jnp.zeros((WIDTH, WIDTH), f32)
    for i in range(HALF - 1):
        state = jnp.where(i < line, advance(lines[i], state), state)
        back = HALF - 1 - i
        grad = jnp.where(back > line, retreat(lines[back], grad), grad)
    for i in range(HALF):
        found[i, :, :WIDTH] = state.astype(bf16)
        back = HALF - 1 - i
        found[back, :, WIDTH:] = grad.astype(bf16)
        if i < HALF - 1:
            state = advance(chips[i], state)
            grad = retreat(chips[back], grad)
    for shift, out in enumerate((o0, o1, o2, o3)):
        out[...] = found[lax.rem(spot + shift, HALF)]


def down_kernel(place, a_ref, b_ref, c_ref, d_ref, keep_ref, got_ref, gkeep_ref, ggot_ref, own_ref, send_ref, slots):
    core = place[0]
    gather_slots(slots, (a_ref, b_ref, c_ref, d_ref), place[1])
    for slot in range(HALF):
        state = slots[slot, :, :WIDTH]
        grad = slots[slot, :, WIDTH:]
        first = jnp.where(core == 0, keep_ref[slot].astype(f32), got_ref[slot].astype(f32))
        second = jnp.where(core == 0, got_ref[slot, :, :WIDTH].astype(f32), keep_ref[slot, :, :WIDTH].astype(f32))
        gsecond = jnp.where(core == 0, ggot_ref[slot].astype(f32), gkeep_ref[slot].astype(f32))
        middle = state.astype(f32) - nn(first[:, :WIDTH].astype(bf16), state) + first[:, WIDTH:]
        gmiddle = grad.astype(f32) - tn(second.astype(bf16), grad) + gsecond
        early = jnp.concatenate([state.astype(f32), gmiddle], axis=1)
        late = jnp.concatenate([middle, grad.astype(f32)], axis=1)
        own_ref[slot] = jnp.where(core == 0, early, late).astype(bf16)
        send_ref[slot] = jnp.where(core == 0, late, early).astype(bf16)


def grads_kernel(
    place, k_ref, q_ref, b_ref, do_ref, nh_ref, nl_ref, y_ref, z_ref, u_ref, own_ref, got_ref,
    dq_ref, dk_ref, dv_ref, db_ref,
):
    step = pl.program_id(0)
    steps_half = HALF // PER_STEP
    tokens = q_ref.shape[0]
    rows = 2 * tokens
    diagonal = eye_mask(rows)
    before = order((rows, rows), 1) < order((rows, rows), 0)
    seen = order((tokens, rows), 1) < 2 * (iota((tokens, rows), 0) + 1)
    seen_t = order((rows, tokens), 0) < 2 * (iota((rows, tokens), 1) + 1)
    for h in range(PER_STEP):
        lanes = slice(h * WIDTH, (h + 1) * WIDTH)
        slot = lax.rem(step, steps_half) * PER_STEP + h
        ends = jnp.where(step < steps_half, got_ref[slot].astype(f32), own_ref[slot].astype(f32)).astype(bf16)
        state, after = ends[:, :WIDTH], ends[:, WIDTH:]
        keys = pick(k_ref, h)
        query = q_ref[:, lanes]
        grad = do_ref[h]
        rate = column(rate_row(b_ref, h), diagonal)
        norm = inverse_norms(keys)
        yh, yl = split(y_ref[h])
        errors = nn(yh, state) + nn(yl, state) - z_ref[h]
        weighted = errors * rate
        d_weighted = -u_ref[h] - norm * nn(keys, after)
        high, low = split(d_weighted * rate)
        back = d_weighted - tn(nh_ref[h], high) - tn(nl_ref[h], high) - tn(nh_ref[h], low)
        scaled = back * rate
        d_rate = jnp.sum(errors * back, axis=1, keepdims=True)
        d_rate = jnp.sum(jnp.where(diagonal, d_rate, 0.0), axis=0, keepdims=True)
        db_ref[h, 0:1, :] = d_rate[:, :tokens]
        db_ref[h, 1:2, :] = d_rate[:, tokens:]
        dv_ref[0, :, lanes] = (-scaled[:tokens]).astype(bf16)
        dv_ref[1, :, lanes] = (-scaled[tokens:]).astype(bf16)
        wh, wl = split(weighted)
        fh, fl = split(scaled)
        wn = (weighted * norm).astype(bf16)
        fn = (scaled * norm).astype(bf16)
        d_scores = jnp.where(seen, -nt(grad, wn), 0.0).astype(bf16)
        dq = nt(grad, state) + nn(d_scores, keys)
        dq_ref[:, lanes] = (dq * SCALE).astype(bf16)
        d_scores_t = jnp.where(seen_t, -nt(wh, grad), 0.0).astype(bf16)
        lower = nt(jnp.concatenate([fh, fl], axis=1), jnp.concatenate([wn, wn], axis=1))
        upper = nt(jnp.concatenate([wh, wl], axis=1), jnp.concatenate([fn, fn], axis=1))
        pairs = jnp.where(before, lower, jnp.where(diagonal, 0.0, upper)).astype(bf16)
        dk = nn(d_scores_t, query) * SCALE - nt(wh, after) + nt(fh, state) - nn(pairs, keys)
        unit = keys.astype(f32) * norm
        dk = norm * (dk - unit * jnp.sum(unit * dk, axis=1, keepdims=True))
        dk_ref[0, :, lanes] = dk[:tokens].astype(bf16)
        dk_ref[1, :, lanes] = dk[tokens:].astype(bf16)


def whole(shape):
    return pl.BlockSpec(shape, lambda *unused: (0,) * len(shape))


def run(kernel, name, place, args, in_specs, outs, out_specs, grid=(1,), scratch=(), cost=None):
    return pl.pallas_call(
        kernel,
        name=name,
        grid_spec=pltpu.PrefetchScalarGridSpec(
            num_scalar_prefetch=1,
            grid=grid,
            in_specs=in_specs,
            out_specs=out_specs,
            scratch_shapes=list(scratch),
        ),
        out_shape=[jax.ShapeDtypeStruct(shape, dtype) for shape, dtype in outs],
        compiler_params=pltpu.CompilerParams(vmem_limit_bytes=40 * 2**20),
        cost_estimate=cost,
    )(place, *args)


def small(kernel, name, place, args, outs, scratch=()):
    return run(
        kernel, name, place, args,
        [whole(a.shape) for a in args],
        outs,
        [whole(shape) for shape, unused in outs],
        scratch=scratch,
    )


def shards(queries, key_input, value_input, beta_rates, out_grad, out_weight):
    tokens = queries.shape[0]
    heads = queries.shape[1] // WIDTH
    rows = 2 * tokens
    model = out_weight.shape[1]
    me = lax.axis_index("ctx")
    place = jnp.stack([me % 2, (me // 2) % HALF, me // (2 * HALF)]).astype(jnp.int32)

    def move(value, target):
        return lax.ppermute(value, "ctx", [(i, target(i)) for i in range(32)])

    def other_core(i):
        return i ^ 1

    def along_x(by):
        return lambda i: (i // 8) * 8 + ((i // 2 + by) % HALF) * 2 + i % 2

    def along_y(by):
        return lambda i: (i + 8 * by) % 32

    steps = heads // PER_STEP
    half_steps = steps // 2

    def block(step, place_ref):
        return lax.rem(step + half_steps * (1 - place_ref[0]), steps)

    kv_spec = pl.BlockSpec((2, tokens, PER_STEP * WIDTH), lambda s, p: (0, 0, block(s, p)))
    q_spec = pl.BlockSpec((tokens, PER_STEP * WIDTH), lambda s, p: (0, block(s, p)))
    b_spec = pl.BlockSpec((PER_STEP, 2, tokens), lambda s, p: (block(s, p), 0, 0))

    def by_step(*shape):
        return pl.BlockSpec((PER_STEP,) + shape, lambda s, p: (s, 0, 0))

    gathered = lax.all_gather(out_grad, "head", axis=0, tiled=True)
    send, keep, core_high, core_low, solved_k, solved_v = run(
        maps_kernel, "maps", place, (key_input, value_input, beta_rates),
        [kv_spec, kv_spec, b_spec],
        [((HALF, WIDTH, 2 * WIDTH), bf16)] * 2 + [((heads, rows, rows), bf16)] * 2
        + [((heads, rows, WIDTH), f32)] * 2,
        [whole((HALF, WIDTH, 2 * WIDTH))] * 2 + [by_step(rows, rows)] * 2 + [by_step(rows, WIDTH)] * 2,
        grid=(steps,),
        scratch=[pltpu.VMEM((rows, rows), jnp.int32)],
        cost=pl.CostEstimate(flops=14_000_000_000, transcendentals=0, bytes_accessed=8_000_000),
    )
    got = move(send, other_core)
    gsend, gkeep, grad, reached = run(
        local_grad_kernel, "local_grad", place,
        (gathered, out_weight, key_input, queries, beta_rates, solved_k),
        [
            whole((tokens, model)),
            pl.BlockSpec((PER_STEP * WIDTH, model), lambda s, p: (block(s, p), 0)),
            kv_spec, q_spec, b_spec, by_step(rows, WIDTH),
        ],
        [((HALF, WIDTH, WIDTH), bf16)] * 2 + [((heads, tokens, WIDTH), bf16), ((heads, rows, WIDTH), f32)],
        [whole((HALF, WIDTH, WIDTH))] * 2 + [by_step(tokens, WIDTH), by_step(rows, WIDTH)],
        grid=(steps,),
        cost=pl.CostEstimate(flops=4_000_000_000, transcendentals=0, bytes_accessed=14_000_000),
    )
    ggot = move(gsend, other_core)
    map_shape = ((WIDTH, 3 * WIDTH), bf16)
    chip = small(pair_kernel, "pair", place, (keep, got, gkeep, ggot), [map_shape] * HALF)
    chip = [chip[0]] + [move(chip[by], along_x(by)) for by in range(1, HALF)]
    slots = pltpu.VMEM((HALF, WIDTH, 3 * WIDTH), bf16)
    (line,) = small(row_kernel, "line", place, chip, [map_shape], [slots])
    lines = [line] + [move(line, along_y(by)) for by in range(1, HALF)]
    ends_shape = ((WIDTH, 2 * WIDTH), bf16)
    ends_slots = pltpu.VMEM((HALF, WIDTH, 2 * WIDTH), bf16)
    ends = small(expand_kernel, "expand", place, chip + lines, [ends_shape] * HALF, [slots, slots, ends_slots])
    ends = [ends[0]] + [move(ends[by], along_x(by)) for by in range(1, HALF)]
    own, passed = small(
        down_kernel, "down", place, ends + [keep, got, gkeep, ggot],
        [((HALF, WIDTH, 2 * WIDTH), bf16)] * 2, [ends_slots],
    )
    taken = move(passed, other_core)
    return tuple(run(
        grads_kernel, "grads", place,
        (key_input, queries, beta_rates, grad, core_high, core_low, solved_k, solved_v, reached, own, taken),
        [
            kv_spec, q_spec, b_spec, by_step(tokens, WIDTH), by_step(rows, rows), by_step(rows, rows),
            by_step(rows, WIDTH), by_step(rows, WIDTH), by_step(rows, WIDTH),
            whole((HALF, WIDTH, 2 * WIDTH)), whole((HALF, WIDTH, 2 * WIDTH)),
        ],
        [
            (queries.shape, bf16), (key_input.shape, bf16), (value_input.shape, bf16), (beta_rates.shape, f32),
        ],
        [q_spec, kv_spec, kv_spec, b_spec],
        grid=(steps,),
        cost=pl.CostEstimate(flops=8_000_000_000, transcendentals=0, bytes_accessed=14_000_000),
    ))


def solution(mesh):
    placed = (
        P("ctx", "head"),
        P(None, "ctx", "head"),
        P(None, "ctx", "head"),
        P("head", None, "ctx"),
        P(("ctx", "head"), None),
        P("head", None),
    )
    return jax.shard_map(
        shards,
        mesh=mesh,
        in_specs=placed,
        out_specs=(
            P("ctx", "head"),
            P(None, "ctx", "head"),
            P(None, "ctx", "head"),
            P("head", None, "ctx"),
        ),
        check_vma=False,
    )
```

```python
import functools

import jax
import jax.numpy as jnp
from jax import lax
from jax.experimental import pallas as pl
from jax.experimental.pallas import tpu as pltpu
from jax.sharding import PartitionSpec as P

WIDTH = 128
HALF = 4
PER_STEP = 4
SCALE = WIDTH ** (-0.5)
bf16 = jnp.bfloat16
f32 = jnp.float32


def dims(left, right):
    return (((left,), (right,)), ((), ()))


def nn(a, b):
    return lax.dot_general(a, b, dims(1, 0), preferred_element_type=f32)


def nt(a, b):
    return lax.dot_general(a, b, dims(1, 1), preferred_element_type=f32)


def tn(a, b):
    return lax.dot_general(a, b, dims(0, 0), preferred_element_type=f32)


def split(x):
    high = x.astype(bf16)
    return high, (x - high.astype(f32)).astype(bf16)


def iota(shape, dim):
    return lax.broadcasted_iota(jnp.int32, shape, dim)


def order(shape, dim):
    index = iota(shape, dim)
    tokens = shape[dim] // 2
    return jnp.where(index < tokens, 2 * index, 2 * (index - tokens) + 1)


def level_table(rows):
    left = order((rows, rows), 0)
    right = order((rows, rows), 1)
    differ = left ^ right
    level = jnp.zeros((rows, rows), jnp.int32)
    for bit in range(1, (rows - 1).bit_length()):
        level = level + (differ >= (1 << bit)).astype(jnp.int32)
    return jnp.where(left > right, level, -1)


def eye_mask(rows):
    return iota((rows, rows), 0) == iota((rows, rows), 1)


def column(row, diagonal):
    return jnp.sum(jnp.where(diagonal, row, 0.0), axis=1, keepdims=True)


def inverse_norms(keys):
    wide = keys.astype(f32)
    return lax.rsqrt(jnp.sum(wide * wide, axis=1, keepdims=True) + 1e-06)


def pick(ref, head, part):
    lanes = slice(head * WIDTH, (head + 1) * WIDTH)
    half = ref.shape[1] // 2
    span = slice(part * half, (part + 1) * half)
    return jnp.concatenate([ref[0, span, lanes], ref[1, span, lanes]], axis=0)


def put(ref, head, part, value):
    lanes = slice(head * WIDTH, (head + 1) * WIDTH)
    half = ref.shape[1] // 2
    span = slice(part * half, (part + 1) * half)
    ref[0, span, lanes] = value[:half]
    ref[1, span, lanes] = value[half:]


def rate_row(ref, head, part):
    half = ref.shape[2] // 2
    span = slice(part * half, (part + 1) * half)
    return jnp.concatenate([ref[head, 0:1, span], ref[head, 1:2, span]], axis=1)


def maps_kernel(place, k_ref, v_ref, b_ref, send_ref, keep_ref, nh_ref, nl_ref, y_ref, z_ref, level_ref):
    step = pl.program_id(0)
    rows = level_ref.shape[0]

    @pl.when(step == 0)
    def _():
        level_ref[...] = level_table(rows)

    diagonal = eye_mask(rows)
    heads = range(PER_STEP)
    chains = [(h, part) for h in heads for part in range(2)]
    every = range(len(chains))
    keys = [pick(k_ref, h, part) for h, part in chains]
    rates = [rate_row(b_ref, h, part) for h, part in chains]
    rate_cols = [column(r, diagonal) for r in rates]
    norms = [inverse_norms(k) for k in keys]
    grams = []
    for i in every:
        raw = nt(keys[i], keys[i])
        norm_row = lax.rsqrt(jnp.sum(jnp.where(diagonal, raw, 0.0), axis=0, keepdims=True) + 1e-06)
        grams.append(jnp.where(level_ref[...] >= 0, raw * norms[i] * norm_row, 0.0))
    systems = [grams[i] * rates[i] for i in every]
    ident = jnp.where(diagonal, 1.0, 0.0).astype(f32)
    inverse = [ident - jnp.where(level_ref[...] == 0, systems[i], 0.0) for i in every]
    for level in range(1, (rows - 1).bit_length()):
        rounded = [t.astype(bf16) for t in inverse]
        inner = [
            nn(jnp.where(level_ref[...] == level, systems[i], 0.0).astype(bf16), rounded[i]).astype(bf16)
            for i in every
        ]
        inverse = [inverse[i] - nn(rounded[i], inner[i]) for i in every]
    rounded = [t.astype(bf16) for t in inverse]
    core_high = [nn(rounded[i], grams[i].astype(bf16)).astype(bf16) for i in every]
    residual = []
    for i in every:
        high, low = split(systems[i])
        residual.append(grams[i] - core_high[i].astype(f32) - nn(high, core_high[i]) - nn(low, core_high[i]))
    core_low = [nn(rounded[i], residual[i].astype(bf16)).astype(bf16) for i in every]
    for i, (h, part) in enumerate(chains):
        nh_ref[h, part] = core_high[i]
        nl_ref[h, part] = core_low[i]

    mapped = [None for h in heads]
    for part in range(2):
        solved = []
        for h in heads:
            i = 2 * h + part
            values = pick(v_ref, h, part)
            both = jnp.concatenate([keys[i].astype(f32) * norms[i], values.astype(f32)], axis=1)
            if part:
                high, low = split(mapped[h])
                both = both - norms[i] * (nn(keys[i], high) + nn(keys[i], low))
            high, low = split(both * rate_cols[i])
            solved.append(both - nn(core_high[i], high) - nn(core_low[i], high) - nn(core_high[i], low))
        for h in heads:
            i = 2 * h + part
            span = slice(part * rows, (part + 1) * rows)
            y_ref[h, span] = solved[h][:, :WIDTH]
            z_ref[h, span] = solved[h][:, WIDTH:]
            high, low = split(solved[h] * (rate_cols[i] * norms[i]))
            found = tn(keys[i], high) + tn(keys[i], low)
            mapped[h] = found if part == 0 else mapped[h] + found
    place_halves(step, send_ref, keep_ref, [m.astype(bf16) for m in mapped])


def place_halves(step, send_ref, keep_ref, values):
    steps_half = HALF // PER_STEP

    @pl.when(step < steps_half)
    def _():
        for h, value in enumerate(values):
            send_ref[step * PER_STEP + h] = value

    @pl.when(step >= steps_half)
    def _():
        for h, value in enumerate(values):
            keep_ref[(step - steps_half) * PER_STEP + h] = value


def local_grad_kernel(
    place, o0, o1, o2, o3, w_ref, k_ref, q_ref, b_ref, y_ref, send_ref, keep_ref, do_ref, u_ref, og_ref
):
    step = pl.program_id(0)

    @pl.when(step == 0)
    def _():
        part = o0.shape[0]
        for shift, ref in enumerate((o0, o1, o2, o3)):
            where = pl.multiple_of(lax.rem(place[3] + HALF - shift, HALF) * part, part)
            og_ref[pl.ds(where, part), :] = ref[...]

    heads = range(PER_STEP)
    tokens = q_ref.shape[0]
    half = tokens // 2
    rows = 2 * half
    diagonal = eye_mask(rows)
    seen = order((rows, half), 0) < 2 * (iota((rows, half), 1) + 1)
    all_grads = nt(og_ref[...], w_ref[...]).astype(bf16)
    grads = [all_grads[:, h * WIDTH : (h + 1) * WIDTH] for h in heads]
    queries = [q_ref[:, h * WIDTH : (h + 1) * WIDTH] for h in heads]
    scaled = [[] for h in heads]
    for part in range(2):
        for h in heads:
            keys = pick(k_ref, h, part)
            score = nt(keys, queries[h]) * (inverse_norms(keys) * SCALE)
            if part == 0:
                score = jnp.concatenate([jnp.where(seen, score[:, :half], 0.0), score[:, half:]], axis=1)
                high, low = split(score)
                reached = nn(high, grads[h]) + nn(low, grads[h])
            else:
                high, low = split(jnp.where(seen, score[:, half:], 0.0))
                reached = nn(high, grads[h][half:]) + nn(low, grads[h][half:])
            u_ref[h, part * rows : (part + 1) * rows] = reached
            scaled[h].append(reached * column(rate_row(b_ref, h, part), diagonal))
    found = []
    for h in heads:
        do_ref[h] = grads[h]
        uh, ul = split(jnp.concatenate(scaled[h], axis=0))
        yh, yl = split(y_ref[h])
        local = tn(queries[h], grads[h]) * SCALE - tn(yh, uh) - tn(yl, uh) - tn(yh, ul)
        found.append(local.astype(bf16))
    place_halves(step, send_ref, keep_ref, found)


def pair_kernel(place, keep_ref, got_ref, gkeep_ref, ggot_ref, *outs):
    core = place[0]
    spot = place[1]
    for shift in range(HALF):
        slot = lax.rem(spot + shift, HALF)
        mine, other = keep_ref[slot].astype(f32), got_ref[slot].astype(f32)
        first = jnp.where(core == 0, mine, other)
        second = jnp.where(core == 0, other, mine)
        mine, other = gkeep_ref[slot].astype(f32), ggot_ref[slot].astype(f32)
        gfirst = jnp.where(core == 0, mine, other)
        gsecond = jnp.where(core == 0, other, mine)
        joined = first + second - nn(second[:, :WIDTH].astype(bf16), first.astype(bf16))
        gjoined = gfirst + gsecond - tn(first[:, :WIDTH].astype(bf16), gsecond.astype(bf16))
        outs[shift][:, : 2 * WIDTH] = joined.astype(bf16)
        outs[shift][:, 2 * WIDTH :] = gjoined.astype(bf16)


def join(first, second):
    forward = first[:, : 2 * WIDTH] + second[:, : 2 * WIDTH]
    forward = forward - nn(second[:, :WIDTH].astype(bf16), first[:, : 2 * WIDTH].astype(bf16))
    backward = first[:, 2 * WIDTH :] + second[:, 2 * WIDTH :]
    backward = backward - tn(first[:, :WIDTH].astype(bf16), second[:, 2 * WIDTH :].astype(bf16))
    return jnp.concatenate([forward, backward], axis=1)


def gather_slots(slots, refs, spot):
    for shift in range(HALF):
        slots[lax.rem(spot + HALF - shift, HALF)] = refs[shift][...]


def row_kernel(place, a_ref, b_ref, c_ref, d_ref, out_ref, slots):
    gather_slots(slots, (a_ref, b_ref, c_ref, d_ref), place[1])
    maps = [slots[i].astype(f32) for i in range(HALF)]
    out_ref[...] = join(join(maps[0], maps[1]), join(maps[2], maps[3])).astype(bf16)


def advance(block, state):
    high, low = split(state)
    moved = nn(block[:, :WIDTH], jnp.concatenate([high, low], axis=1))
    return state - moved[:, :WIDTH] - moved[:, WIDTH:] + block[:, WIDTH : 2 * WIDTH].astype(f32)


def retreat(block, grad):
    high, low = split(grad)
    moved = tn(block[:, :WIDTH], jnp.concatenate([high, low], axis=1))
    return grad - moved[:, :WIDTH] - moved[:, WIDTH:] + block[:, 2 * WIDTH :].astype(f32)


def expand_kernel(place, a_ref, b_ref, c_ref, d_ref, e_ref, f_ref, g_ref, h_ref, o0, o1, o2, o3, chips, lines, found):
    spot, line = place[1], place[2]
    gather_slots(chips, (a_ref, b_ref, c_ref, d_ref), spot)
    gather_slots(lines, (e_ref, f_ref, g_ref, h_ref), line)
    state = jnp.zeros((WIDTH, WIDTH), f32)
    grad = jnp.zeros((WIDTH, WIDTH), f32)
    for i in range(HALF - 1):
        state = jnp.where(i < line, advance(lines[i], state), state)
        back = HALF - 1 - i
        grad = jnp.where(back > line, retreat(lines[back], grad), grad)
    for i in range(HALF):
        found[i, :, :WIDTH] = state.astype(bf16)
        back = HALF - 1 - i
        found[back, :, WIDTH:] = grad.astype(bf16)
        if i < HALF - 1:
            state = advance(chips[i], state)
            grad = retreat(chips[back], grad)
    for shift, out in enumerate((o0, o1, o2, o3)):
        out[...] = found[lax.rem(spot + shift, HALF)]


def down_kernel(place, a_ref, b_ref, c_ref, d_ref, keep_ref, got_ref, gkeep_ref, ggot_ref, own_ref, send_ref, slots):
    core = place[0]
    gather_slots(slots, (a_ref, b_ref, c_ref, d_ref), place[1])
    for slot in range(HALF):
        state = slots[slot, :, :WIDTH]
        grad = slots[slot, :, WIDTH:]
        first = jnp.where(core == 0, keep_ref[slot].astype(f32), got_ref[slot].astype(f32))
        second = jnp.where(core == 0, got_ref[slot, :, :WIDTH].astype(f32), keep_ref[slot, :, :WIDTH].astype(f32))
        gsecond = jnp.where(core == 0, ggot_ref[slot].astype(f32), gkeep_ref[slot].astype(f32))
        middle = state.astype(f32) - nn(first[:, :WIDTH].astype(bf16), state) + first[:, WIDTH:]
        gmiddle = grad.astype(f32) - tn(second.astype(bf16), grad) + gsecond
        early = jnp.concatenate([state.astype(f32), gmiddle], axis=1)
        late = jnp.concatenate([middle, grad.astype(f32)], axis=1)
        own_ref[slot] = jnp.where(core == 0, early, late).astype(bf16)
        send_ref[slot] = jnp.where(core == 0, late, early).astype(bf16)


def grads_kernel(
    place, k_ref, q_ref, b_ref, do_ref, nh_ref, nl_ref, y_ref, z_ref, u_ref, own_ref, got_ref,
    dq_ref, dk_ref, dv_ref, db_ref,
):
    step = pl.program_id(0)
    steps_half = HALF // PER_STEP
    heads = range(PER_STEP)
    parts = range(2)
    both = [(h, p) for h in heads for p in parts]
    tokens = q_ref.shape[0]
    half = tokens // 2
    rows = 2 * half
    diagonal = eye_mask(rows)
    before = order((rows, rows), 1) < order((rows, rows), 0)
    seen = order((half, rows), 1) < 2 * (iota((half, rows), 0) + 1)
    seen_t = order((rows, half), 0) < 2 * (iota((rows, half), 1) + 1)
    spans = [slice(p * rows, (p + 1) * rows) for p in parts]

    state, after = [], []
    for h in heads:
        slot = lax.rem(step, steps_half) * PER_STEP + h
        ends = jnp.where(step < steps_half, got_ref[slot].astype(f32), own_ref[slot].astype(f32)).astype(bf16)
        state.append(ends[:, :WIDTH])
        after.append(ends[:, WIDTH:])
    keys = {(h, p): pick(k_ref, h, p) for h, p in both}
    rate = {(h, p): column(rate_row(b_ref, h, p), diagonal) for h, p in both}
    norm = {c: inverse_norms(keys[c]) for c in both}
    query = [q_ref[:, h * WIDTH : (h + 1) * WIDTH] for h in heads]

    ahead = {(h, p): -u_ref[h, spans[p]] - norm[h, p] * nn(keys[h, p], after[h]) for h, p in both}
    back = {}
    for p in (1, 0):
        if p == 0:
            passed = {h: split(back[h, 1] * (rate[h, 1] * norm[h, 1])) for h in heads}
            passed = {h: split(tn(keys[h, 1], passed[h][0]) + tn(keys[h, 1], passed[h][1])) for h in heads}
            for h in heads:
                ahead[h, 0] = ahead[h, 0] - norm[h, 0] * (nn(keys[h, 0], passed[h][0]) + nn(keys[h, 0], passed[h][1]))
        pieces = {h: split(ahead[h, p] * rate[h, p]) for h in heads}
        for h in heads:
            high, low = pieces[h]
            back[h, p] = ahead[h, p] - tn(nh_ref[h, p], high) - tn(nl_ref[h, p], high) - tn(nh_ref[h, p], low)
    errors = {}
    for h, p in both:
        yh, yl = split(y_ref[h, spans[p]])
        errors[h, p] = nn(yh, state[h]) + nn(yl, state[h]) - z_ref[h, spans[p]]
    weighted = {c: errors[c] * rate[c] for c in both}
    scaled = {c: back[c] * rate[c] for c in both}
    for h, p in both:
        d_rate = jnp.sum(errors[h, p] * back[h, p], axis=1, keepdims=True)
        d_rate = jnp.sum(jnp.where(diagonal, d_rate, 0.0), axis=0, keepdims=True)
        db_ref[h, 0:1, p * half : (p + 1) * half] = d_rate[:, :half]
        db_ref[h, 1:2, p * half : (p + 1) * half] = d_rate[:, half:]
        put(dv_ref, h, p, (-scaled[h, p]).astype(bf16))
    ws = {c: split(weighted[c]) for c in both}
    fs = {c: split(scaled[c]) for c in both}
    wn = [jnp.concatenate([(weighted[h, p] * norm[h, p]).astype(bf16) for p in parts], axis=0) for h in heads]
    fn = [jnp.concatenate([(scaled[h, p] * norm[h, p]).astype(bf16) for p in parts], axis=0) for h in heads]
    all_keys = [jnp.concatenate([keys[h, p] for p in parts], axis=0) for h in heads]

    score = [nt(do_ref[h], wn[h]) for h in heads]
    score_t = {(h, p): nt(ws[h, p][0], do_ref[h] if p == 0 else do_ref[h, half:]) for h, p in both}
    lower, upper = {}, {}
    for h, p in both:
        first = jnp.concatenate(ws[h, p], axis=1)
        second = jnp.concatenate(fs[h, p], axis=1)
        wn2 = jnp.concatenate([wn[h], wn[h]], axis=1)
        fn2 = jnp.concatenate([fn[h], fn[h]], axis=1)
        upper[h, p] = nt(first, fn2 if p == 0 else fn2[rows:])
        lower[h, p] = nt(second, wn2[:rows] if p == 0 else wn2)
    pairs, reads = {}, {}
    for h, p in both:
        if p == 0:
            own = jnp.where(before, lower[h, p], jnp.where(diagonal, 0.0, upper[h, p][:, :rows]))
            pairs[h, p] = jnp.concatenate([own, upper[h, p][:, rows:]], axis=1).astype(bf16)
            masked = jnp.concatenate(
                [jnp.where(seen_t, score_t[h, p][:, :half], 0.0), score_t[h, p][:, half:]], axis=1
            )
            reads[h, p] = nn(masked.astype(bf16), query[h])
        else:
            own = jnp.where(before, lower[h, p][:, rows:], jnp.where(diagonal, 0.0, upper[h, p]))
            pairs[h, p] = jnp.concatenate([lower[h, p][:, :rows], own], axis=1).astype(bf16)
            reads[h, p] = nn(jnp.where(seen_t, score_t[h, p], 0.0).astype(bf16), query[h][half:])
    for h in heads:
        masked = jnp.concatenate([
            jnp.concatenate([jnp.where(seen, score[h][:half, :rows], 0.0), jnp.zeros((half, rows), f32)], axis=1),
            jnp.concatenate([score[h][half:, :rows], jnp.where(seen, score[h][half:, rows:], 0.0)], axis=1),
        ], axis=0).astype(bf16)
        dq = nt(do_ref[h], state[h]) - nn(masked, all_keys[h])
        dq_ref[:, h * WIDTH : (h + 1) * WIDTH] = (dq * SCALE).astype(bf16)
    for h, p in both:
        dk = nt(fs[h, p][0], state[h]) - reads[h, p] * SCALE - nt(ws[h, p][0], after[h]) - nn(pairs[h, p], all_keys[h])
        unit = keys[h, p].astype(f32) * norm[h, p]
        dk = norm[h, p] * (dk - unit * jnp.sum(unit * dk, axis=1, keepdims=True))
        put(dk_ref, h, p, dk.astype(bf16))


def whole(shape):
    return pl.BlockSpec(shape, lambda *unused: (0,) * len(shape))


def run(kernel, name, place, args, in_specs, outs, out_specs, grid=(1,), scratch=(), cost=None, vmem=56):
    return pl.pallas_call(
        kernel,
        name=name,
        grid_spec=pltpu.PrefetchScalarGridSpec(
            num_scalar_prefetch=1,
            grid=grid,
            in_specs=in_specs,
            out_specs=out_specs,
            scratch_shapes=list(scratch),
        ),
        out_shape=[jax.ShapeDtypeStruct(shape, dtype) for shape, dtype in outs],
        compiler_params=pltpu.CompilerParams(vmem_limit_bytes=vmem * 2**20),
        cost_estimate=cost,
    )(place, *args)


def small(kernel, name, place, args, outs, scratch=()):
    return run(
        kernel, name, place, args,
        [whole(a.shape) for a in args],
        outs,
        [whole(shape) for shape, unused in outs],
        scratch=scratch,
        vmem=16,
    )


def shards(queries, key_input, value_input, beta_rates, out_grad, out_weight):
    tokens = queries.shape[0]
    heads = queries.shape[1] // WIDTH
    rows = 2 * tokens
    model = out_weight.shape[1]
    key_input, value_input, queries, out_weight, beta_rates = (
        pltpu.with_memory_space_constraint(a, pltpu.HBM)
        for a in (key_input, value_input, queries, out_weight, beta_rates)
    )
    me = lax.axis_index("ctx")
    place = jnp.stack([me % 2, (me // 2) % HALF, me // (2 * HALF), lax.axis_index("head")]).astype(jnp.int32)

    def move(value, target):
        return lax.ppermute(value, "ctx", [(i, target(i)) for i in range(32)])

    def other_core(i):
        return i ^ 1

    def along_x(by):
        return lambda i: (i // 8) * 8 + ((i // 2 + by) % HALF) * 2 + i % 2

    def along_y(by):
        return lambda i: (i + 8 * by) % 32

    steps = heads // PER_STEP
    half_steps = steps // 2

    def block(step, place_ref):
        return lax.rem(step + half_steps * (1 - place_ref[0]), steps)

    kv_spec = pl.BlockSpec((2, tokens, PER_STEP * WIDTH), lambda s, p: (0, 0, block(s, p)))
    q_spec = pl.BlockSpec((tokens, PER_STEP * WIDTH), lambda s, p: (0, block(s, p)))
    b_spec = pl.BlockSpec((PER_STEP, 2, tokens), lambda s, p: (block(s, p), 0, 0))

    def by_step(*shape):
        return pl.BlockSpec((PER_STEP,) + shape, lambda s, p: (s,) + (0,) * len(shape))

    gathered = [out_grad] + [
        lax.ppermute(out_grad, "head", [(i, (i + by) % HALF) for i in range(HALF)]) for by in (1, 3, 2)
    ]
    gathered = [gathered[0], gathered[1], gathered[3], gathered[2]]
    send, keep, core_high, core_low, solved_k, solved_v = run(
        maps_kernel, "maps", place, (key_input, value_input, beta_rates),
        [kv_spec, kv_spec, b_spec],
        [((HALF, WIDTH, 2 * WIDTH), bf16)] * 2 + [((heads, 2, tokens, tokens), bf16)] * 2
        + [((heads, rows, WIDTH), f32)] * 2,
        [whole((HALF, WIDTH, 2 * WIDTH))] * 2 + [by_step(2, tokens, tokens)] * 2 + [by_step(rows, WIDTH)] * 2,
        grid=(steps,),
        scratch=[pltpu.VMEM((tokens, tokens), jnp.int32)],
        vmem=24,
        cost=pl.CostEstimate(flops=14_000_000_000, transcendentals=0, bytes_accessed=8_000_000),
    )
    got = move(send, other_core)
    gsend, gkeep, grad, reached = run(
        local_grad_kernel, "local_grad", place,
        (*gathered, out_weight, key_input, queries, beta_rates, solved_k),
        [
            *[whole(out_grad.shape)] * HALF,
            pl.BlockSpec((PER_STEP * WIDTH, model), lambda s, p: (block(s, p), 0)),
            kv_spec, q_spec, b_spec, by_step(rows, WIDTH),
        ],
        [((HALF, WIDTH, WIDTH), bf16)] * 2 + [((heads, tokens, WIDTH), bf16), ((heads, rows, WIDTH), f32)],
        [whole((HALF, WIDTH, WIDTH))] * 2 + [by_step(tokens, WIDTH), by_step(rows, WIDTH)],
        grid=(steps,),
        scratch=[pltpu.VMEM((tokens, model), bf16)],
        vmem=32,
        cost=pl.CostEstimate(flops=4_000_000_000, transcendentals=0, bytes_accessed=14_000_000),
    )
    ggot = move(gsend, other_core)
    map_shape = ((WIDTH, 3 * WIDTH), bf16)
    chip = small(pair_kernel, "pair", place, (keep, got, gkeep, ggot), [map_shape] * HALF)
    chip = [chip[0]] + [move(chip[by], along_x(by)) for by in range(1, HALF)]
    slots = pltpu.VMEM((HALF, WIDTH, 3 * WIDTH), bf16)
    (line,) = small(row_kernel, "line", place, chip, [map_shape], [slots])
    lines = [line] + [move(line, along_y(by)) for by in range(1, HALF)]
    ends_shape = ((WIDTH, 2 * WIDTH), bf16)
    ends_slots = pltpu.VMEM((HALF, WIDTH, 2 * WIDTH), bf16)
    ends = small(expand_kernel, "expand", place, chip + lines, [ends_shape] * HALF, [slots, slots, ends_slots])
    ends = [ends[0]] + [move(ends[by], along_x(by)) for by in range(1, HALF)]
    own, passed = small(
        down_kernel, "down", place, ends + [keep, got, gkeep, ggot],
        [((HALF, WIDTH, 2 * WIDTH), bf16)] * 2, [ends_slots],
    )
    taken = move(passed, other_core)
    return tuple(run(
        grads_kernel, "grads", place,
        (key_input, queries, beta_rates, grad, core_high, core_low, solved_k, solved_v, reached, own, taken),
        [
            kv_spec, q_spec, b_spec, by_step(tokens, WIDTH), by_step(2, tokens, tokens), by_step(2, tokens, tokens),
            by_step(rows, WIDTH), by_step(rows, WIDTH), by_step(rows, WIDTH),
            whole((HALF, WIDTH, 2 * WIDTH)), whole((HALF, WIDTH, 2 * WIDTH)),
        ],
        [
            (queries.shape, bf16), (key_input.shape, bf16), (value_input.shape, bf16), (beta_rates.shape, f32),
        ],
        [q_spec, kv_spec, kv_spec, b_spec],
        grid=(steps,),
        vmem=24,
        cost=pl.CostEstimate(flops=8_000_000_000, transcendentals=0, bytes_accessed=14_000_000),
    ))


def solution(mesh):
    placed = (
        P("ctx", "head"),
        P(None, "ctx", "head"),
        P(None, "ctx", "head"),
        P("head", None, "ctx"),
        P(("ctx", "head"), None),
        P("head", None),
    )
    return jax.shard_map(
        shards,
        mesh=mesh,
        in_specs=placed,
        out_specs=(
            P("ctx", "head"),
            P(None, "ctx", "head"),
            P(None, "ctx", "head"),
            P("head", None, "ctx"),
        ),
        check_vma=False,
    )
```

```python
import functools

import jax
import jax.numpy as jnp
from jax import lax
from jax.experimental import pallas as pl
from jax.experimental.pallas import tpu as pltpu
from jax.sharding import PartitionSpec as P

WIDTH = 128
HALF = 4
MAPS_HEADS = 8
LOCAL_HEADS = 8
PREP_HEADS = 8
GRADS_HEADS = 8
SCALE = WIDTH ** (-0.5)
bf16 = jnp.bfloat16
f32 = jnp.float32


def dims(left, right):
    return (((left,), (right,)), ((), ()))


def nn(a, b):
    return lax.dot_general(a, b, dims(1, 0), preferred_element_type=f32)


def nt(a, b):
    return lax.dot_general(a, b, dims(1, 1), preferred_element_type=f32)


def tn(a, b):
    return lax.dot_general(a, b, dims(0, 0), preferred_element_type=f32)


def split(x):
    high = x.astype(bf16)
    return high, (x - high.astype(f32)).astype(bf16)


def iota(shape, dim):
    return lax.broadcasted_iota(jnp.int32, shape, dim)


def order(shape, dim):
    index = iota(shape, dim)
    tokens = shape[dim] // 2
    return jnp.where(index < tokens, 2 * index, 2 * (index - tokens) + 1)


def level_table(rows):
    left = order((rows, rows), 0)
    right = order((rows, rows), 1)
    differ = left ^ right
    level = jnp.zeros((rows, rows), jnp.int32)
    for bit in range(1, (rows - 1).bit_length()):
        level = level + (differ >= (1 << bit)).astype(jnp.int32)
    return jnp.where(left > right, level, -1)


def eye_mask(rows):
    return iota((rows, rows), 0) == iota((rows, rows), 1)


def column(row, diagonal):
    return jnp.sum(jnp.where(diagonal, row, 0.0), axis=1, keepdims=True)


def inverse_norms(keys):
    wide = keys.astype(f32)
    return lax.rsqrt(jnp.sum(wide * wide, axis=1, keepdims=True) + 1e-06)


def pick(ref, head, part):
    lanes = slice(head * WIDTH, (head + 1) * WIDTH)
    half = ref.shape[1] // 2
    span = slice(part * half, (part + 1) * half)
    return jnp.concatenate([ref[0, span, lanes], ref[1, span, lanes]], axis=0)


def put(ref, head, part, value):
    lanes = slice(head * WIDTH, (head + 1) * WIDTH)
    half = ref.shape[1] // 2
    span = slice(part * half, (part + 1) * half)
    ref[0, span, lanes] = value[:half]
    ref[1, span, lanes] = value[half:]


def rate_row(ref, head, part):
    half = ref.shape[2] // 2
    span = slice(part * half, (part + 1) * half)
    return jnp.concatenate([ref[head, 0:1, span], ref[head, 1:2, span]], axis=1)


def here():
    me = lax.axis_index("ctx")
    return me % 2, lax.rem(me // 2, HALF), me // (2 * HALF)


def maps_kernel(
    k_ref, v_ref, q_ref, b_ref, w_ref, send_ref, keep_ref, nh_ref, nl_ref, yh_ref, yl_ref, z_ref, sh_ref, sl_ref,
    rh_ref, rl_ref, ph_ref, pl_ref, near_ref, near_sem,
):
    fetch = pltpu.make_async_copy(w_ref, near_ref, near_sem)
    fetch.start()
    rows = k_ref.shape[1]
    level_of = level_table(rows)
    diagonal = eye_mask(rows)
    heads = range(MAPS_HEADS)
    chains = [(h, part) for h in heads for part in range(2)]
    every = range(len(chains))
    keys = [pick(k_ref, h, part) for h, part in chains]
    rates = [rate_row(b_ref, h, part) for h, part in chains]
    rate_cols = [column(r, diagonal) for r in rates]
    norms = [inverse_norms(k) for k in keys]
    grams = []
    for i in every:
        raw = nt(keys[i], keys[i])
        norm_row = lax.rsqrt(jnp.sum(jnp.where(diagonal, raw, 0.0), axis=0, keepdims=True) + 1e-06)
        grams.append(jnp.where(level_of >= 0, raw * norms[i] * norm_row, 0.0))
    half = rows // 2
    seen = order((rows, half), 0) < 2 * (iota((rows, half), 1) + 1)
    scores = {}
    for i, (h, part) in enumerate(chains):
        query = q_ref[:, h * WIDTH : (h + 1) * WIDTH]
        score = nt(keys[i], query) * (norms[i] * SCALE)
        if part == 0:
            score = jnp.concatenate([jnp.where(seen, score[:, :half], 0.0), score[:, half:]], axis=1)
        else:
            score = jnp.concatenate([jnp.zeros((rows, half), f32), jnp.where(seen, score[:, half:], 0.0)], axis=1)
        scores[h, part] = split(score)
        sh_ref[h, part], sl_ref[h, part] = scores[h, part]
    core = list(grams)
    for level in range((rows - 1).bit_length()):
        joins = [jnp.where(level_of == level, core[i] * rates[i], 0.0).astype(bf16) for i in every]
        core = [core[i] - nn(joins[i], core[i].astype(bf16)) for i in every]
    core_high = [c.astype(bf16) for c in core]
    residual = []
    for i in every:
        high, low = split(grams[i] * rates[i])
        residual.append(grams[i] - core_high[i].astype(f32) - nn(high, core_high[i]) - nn(low, core_high[i]))
    core_low = [
        (residual[i] - nn(core_high[i], (rate_cols[i] * residual[i]).astype(bf16))).astype(bf16) for i in every
    ]
    for i, (h, part) in enumerate(chains):
        nh_ref[h, part] = core_high[i]
        nl_ref[h, part] = core_low[i]

    mapped = [None for h in heads]
    weighted, adjoint = {}, {}
    for part in range(2):
        now = [2 * h + part for h in heads]
        late = [2 * h + 1 - part for h in heads]
        both = [
            jnp.concatenate([keys[i].astype(f32) * norms[i], pick(v_ref, h, part).astype(f32)], axis=1)
            for h, i in enumerate(now)
        ]
        ahead = [keys[i].astype(f32) * norms[i] for i in late]
        if part:
            pieces = [split(m) for m in mapped]
            both = [
                both[h] - norms[i] * (nn(keys[i], pieces[h][0]) + nn(keys[i], pieces[h][1])) for h, i in enumerate(now)
            ]
            pieces = [split(adjoint[h] * (rate_cols[i + 1] * norms[i + 1])) for h, i in enumerate(late)]
            passed = [tn(keys[i + 1], pieces[h][0]) + tn(keys[i + 1], pieces[h][1]) for h, i in enumerate(late)]
            pieces = [split(p) for p in passed]
            ahead = [
                ahead[h] - norms[i] * (nn(keys[i], pieces[h][0]) + nn(keys[i], pieces[h][1]))
                for h, i in enumerate(late)
            ]
        pieces = [split(both[h] * rate_cols[i]) for h, i in enumerate(now)]
        solved = [
            both[h] - nn(core_high[i], pieces[h][0]) - nn(core_low[i], pieces[h][0]) - nn(core_high[i], pieces[h][1])
            for h, i in enumerate(now)
        ]
        pieces = [split(ahead[h] * rate_cols[i]) for h, i in enumerate(late)]
        adjoint = [
            ahead[h] - tn(core_high[i], pieces[h][0]) - tn(core_low[i], pieces[h][0]) - tn(core_high[i], pieces[h][1])
            for h, i in enumerate(late)
        ]
        for h, i in enumerate(now):
            yh_ref[h, part], yl_ref[h, part] = split(solved[h][:, :WIDTH])
            z_ref[h, part] = solved[h][:, WIDTH:]
            weighted[h, part] = split(solved[h][:, :WIDTH] * rate_cols[i])
        pieces = [split(solved[h] * (rate_cols[i] * norms[i])) for h, i in enumerate(now)]
        found = [tn(keys[i], pieces[h][0]) + tn(keys[i], pieces[h][1]) for h, i in enumerate(now)]
        mapped = [found[h] if part == 0 else mapped[h] + found[h] for h in heads]
        for h in heads:
            ph_ref[h, 1 - part], pl_ref[h, 1 - part] = split(adjoint[h])
    place_halves(send_ref, keep_ref, mapped)

    stacked = [
        [jnp.concatenate([pair[h, 0][k], pair[h, 1][k]], axis=0) for pair in (scores, weighted) for k in range(2)]
        for h in heads
    ]
    taken = [tn(sh, wh) + tn(sl, wh) + tn(sh, wl) for sh, sl, wh, wl in stacked]
    for h in heads:
        rh_ref[h], rl_ref[h] = split(q_ref[:, h * WIDTH : (h + 1) * WIDTH].astype(f32) * SCALE - taken[h])
    fetch.wait()


def place_halves(send_ref, keep_ref, values):
    first = here()[0] == 0
    for slot in range(HALF):
        low, high = values[slot], values[HALF + slot]
        keep_ref[slot] = jnp.where(first, low, high).astype(bf16)
        send_ref[slot] = jnp.where(first, high, low).astype(bf16)


def local_grad_kernel(o0, o1, o2, o3, w_ref, rh_ref, rl_ref, send_ref, keep_ref, do_ref, og_ref):
    part = o0.shape[0]
    for shift, ref in enumerate((o0, o1, o2, o3)):
        where = pl.multiple_of(lax.rem(lax.axis_index("head") + HALF - shift, HALF) * part, part)
        og_ref[pl.ds(where, part), :] = ref[...]
    grads = nt(og_ref[...], w_ref[...]).astype(bf16)
    found = []
    for h in range(LOCAL_HEADS):
        grad = grads[:, h * WIDTH : (h + 1) * WIDTH]
        do_ref[h] = grad
        found.append(tn(rh_ref[h], grad) + tn(rl_ref[h], grad))
    place_halves(send_ref, keep_ref, found)


def prep_kernel(k_ref, b_ref, do_ref, nh_ref, nl_ref, sh_ref, sl_ref, u_ref):
    heads = range(PREP_HEADS)
    rows = k_ref.shape[1]
    diagonal = eye_mask(rows)
    reached = {
        (h, part): nn(sh_ref[h, part], do_ref[h]) + nn(sl_ref[h, part], do_ref[h]) for part in (1, 0) for h in heads
    }
    keys = {(h, part): pick(k_ref, h, part) for part in (1, 0) for h in heads}
    norms = {c: inverse_norms(keys[c]) for c in keys}
    rates = {(h, part): column(rate_row(b_ref, h, part), diagonal) for part in (1, 0) for h in heads}
    solved = [None]*8
    for part in (1, 0):
        ahead = [reached[h, part] for h in heads]
        if part == 0:
            pieces = [split(solved[h] * (rates[h, 1] * norms[h, 1])) for h in heads]
            passed = [tn(keys[h, 1], pieces[h][0]) + tn(keys[h, 1], pieces[h][1]) for h in heads]
            pieces = [split(p) for p in passed]
            ahead = [
                ahead[h] - norms[h, 0] * (nn(keys[h, 0], pieces[h][0]) + nn(keys[h, 0], pieces[h][1])) for h in heads
            ]
        pieces = [split(ahead[h] * rates[h, part]) for h in heads]
        solved = [
            ahead[h] - tn(nh_ref[h, part], pieces[h][0]) - tn(nl_ref[h, part], pieces[h][0])
            - tn(nh_ref[h, part], pieces[h][1])
            for h in heads
        ]
        for h in heads:
            u_ref[h, part] = solved[h]


def pair_kernel(keep_ref, got_ref, gkeep_ref, ggot_ref, *outs):
    core, spot, unused = here()
    for shift in range(HALF):
        slot = lax.rem(spot + shift, HALF)
        mine, other = keep_ref[slot].astype(f32), got_ref[slot].astype(f32)
        first = jnp.where(core == 0, mine, other)
        second = jnp.where(core == 0, other, mine)
        mine, other = gkeep_ref[slot].astype(f32), ggot_ref[slot].astype(f32)
        gfirst = jnp.where(core == 0, mine, other)
        gsecond = jnp.where(core == 0, other, mine)
        joined = first + second - nn(second[:, :WIDTH].astype(bf16), first.astype(bf16))
        gjoined = gfirst + gsecond - tn(first[:, :WIDTH].astype(bf16), gsecond.astype(bf16))
        outs[shift][:, : 2 * WIDTH] = joined.astype(bf16)
        outs[shift][:, 2 * WIDTH :] = gjoined.astype(bf16)


def join(first, second):
    forward = first[:, : 2 * WIDTH] + second[:, : 2 * WIDTH]
    forward = forward - nn(second[:, :WIDTH].astype(bf16), first[:, : 2 * WIDTH].astype(bf16))
    backward = first[:, 2 * WIDTH :] + second[:, 2 * WIDTH :]
    backward = backward - tn(first[:, :WIDTH].astype(bf16), second[:, 2 * WIDTH :].astype(bf16))
    return jnp.concatenate([forward, backward], axis=1)


def gather_slots(slots, refs, spot):
    for shift in range(HALF):
        slots[lax.rem(spot + HALF - shift, HALF)] = refs[shift][...]


def row_kernel(a_ref, b_ref, c_ref, d_ref, out_ref, slots):
    gather_slots(slots, (a_ref, b_ref, c_ref, d_ref), here()[1])
    maps = [slots[i].astype(f32) for i in range(HALF)]
    out_ref[...] = join(join(maps[0], maps[1]), join(maps[2], maps[3])).astype(bf16)


def advance(block, state):
    high, low = split(state)
    moved = nn(block[:, :WIDTH], jnp.concatenate([high, low], axis=1))
    return state - moved[:, :WIDTH] - moved[:, WIDTH:] + block[:, WIDTH : 2 * WIDTH].astype(f32)


def retreat(block, grad):
    high, low = split(grad)
    moved = tn(block[:, :WIDTH], jnp.concatenate([high, low], axis=1))
    return grad - moved[:, :WIDTH] - moved[:, WIDTH:] + block[:, 2 * WIDTH :].astype(f32)


def expand_kernel(a_ref, b_ref, c_ref, d_ref, e_ref, f_ref, g_ref, h_ref, o0, o1, o2, o3, chips, lines, found):
    unused, spot, line = here()
    gather_slots(chips, (a_ref, b_ref, c_ref, d_ref), spot)
    gather_slots(lines, (e_ref, f_ref, g_ref, h_ref), line)
    state = jnp.zeros((WIDTH, WIDTH), f32)
    grad = jnp.zeros((WIDTH, WIDTH), f32)
    for i in range(HALF - 1):
        state = jnp.where(i < line, advance(lines[i], state), state)
        back = HALF - 1 - i
        grad = jnp.where(back > line, retreat(lines[back], grad), grad)
    for i in range(HALF):
        found[i, :, :WIDTH] = state.astype(bf16)
        back = HALF - 1 - i
        found[back, :, WIDTH:] = grad.astype(bf16)
        if i < HALF - 1:
            state = advance(chips[i], state)
            grad = retreat(chips[back], grad)
    for shift, out in enumerate((o0, o1, o2, o3)):
        out[...] = found[lax.rem(spot + shift, HALF)]


def down_kernel(a_ref, b_ref, c_ref, d_ref, keep_ref, got_ref, gkeep_ref, ggot_ref, own_ref, send_ref, slots):
    core, spot, unused = here()
    gather_slots(slots, (a_ref, b_ref, c_ref, d_ref), spot)
    for slot in range(HALF):
        state = slots[slot, :, :WIDTH]
        grad = slots[slot, :, WIDTH:]
        first = jnp.where(core == 0, keep_ref[slot].astype(f32), got_ref[slot].astype(f32))
        second = jnp.where(core == 0, got_ref[slot, :, :WIDTH].astype(f32), keep_ref[slot, :, :WIDTH].astype(f32))
        gsecond = jnp.where(core == 0, ggot_ref[slot].astype(f32), gkeep_ref[slot].astype(f32))
        middle = state.astype(f32) - nn(first[:, :WIDTH].astype(bf16), state) + first[:, WIDTH:]
        gmiddle = grad.astype(f32) - tn(second.astype(bf16), grad) + gsecond
        early = jnp.concatenate([state.astype(f32), gmiddle], axis=1)
        late = jnp.concatenate([middle, grad.astype(f32)], axis=1)
        own_ref[slot] = jnp.where(core == 0, early, late).astype(bf16)
        send_ref[slot] = jnp.where(core == 0, late, early).astype(bf16)


def grads_kernel(
    k_ref, q_ref, b_ref, do_ref, yh_ref, yl_ref, z_ref, ph_ref, pl_ref, u_ref, own_ref, got_ref,
    dq_ref, dk_ref, dv_ref, db_ref,
):
    step = pl.program_id(0)
    core = here()[0]
    heads = range(GRADS_HEADS)
    parts = range(2)
    both = [(h, p) for h in heads for p in parts]
    tokens = q_ref.shape[0]
    half = tokens // 2
    rows = 2 * half
    diagonal = eye_mask(rows)
    before = order((rows, rows), 1) < order((rows, rows), 0)
    seen = order((half, rows), 1) < 2 * (iota((half, rows), 0) + 1)
    seen_t = order((rows, half), 0) < 2 * (iota((rows, half), 1) + 1)
    state, after = [], []
    for h in heads:
        head = step * GRADS_HEADS + h
        slot = lax.rem(head, HALF)
        mine = head // HALF == core
        ends = jnp.where(mine, own_ref[slot].astype(f32), got_ref[slot].astype(f32)).astype(bf16)
        state.append(ends[:, :WIDTH])
        after.append(ends[:, WIDTH:])
    keys = {(h, p): pick(k_ref, h, p) for h, p in both}
    rate = {(h, p): column(rate_row(b_ref, h, p), diagonal) for h, p in both}
    norm = {c: inverse_norms(keys[c]) for c in both}
    query = [q_ref[:, h * WIDTH : (h + 1) * WIDTH] for h in heads]

    errors, back = {}, {}
    for h, p in both:
        errors[h, p] = nn(yh_ref[h, p], state[h]) + nn(yl_ref[h, p], state[h]) - z_ref[h, p]
        back[h, p] = -u_ref[h, p] - nn(ph_ref[h, p], after[h]) - nn(pl_ref[h, p], after[h])
    weighted = {c: errors[c] * rate[c] for c in both}
    scaled = {c: back[c] * rate[c] for c in both}
    d_rate = {c: jnp.sum(errors[c] * back[c], axis=1, keepdims=True) for c in both}
    d_rate = {c: jnp.sum(jnp.where(diagonal, d_rate[c], 0.0), axis=0, keepdims=True) for c in both}
    for h, p in both:
        db_ref[h, 0:1, p * half : (p + 1) * half] = d_rate[h, p][:, :half]
        db_ref[h, 1:2, p * half : (p + 1) * half] = d_rate[h, p][:, half:]
        put(dv_ref, h, p, (-scaled[h, p]).astype(bf16))
    ws = {c: split(weighted[c]) for c in both}
    fs = {c: split(scaled[c]) for c in both}
    wn = [jnp.concatenate([(weighted[h, p] * norm[h, p]).astype(bf16) for p in parts], axis=0) for h in heads]
    fn = [jnp.concatenate([(scaled[h, p] * norm[h, p]).astype(bf16) for p in parts], axis=0) for h in heads]
    all_keys = [jnp.concatenate([keys[h, p] for p in parts], axis=0) for h in heads]

    score = [nt(do_ref[h], wn[h]) for h in heads]
    score_t = {(h, p): nt(ws[h, p][0], do_ref[h] if p == 0 else do_ref[h, half:]) for h, p in both}
    lower, upper = {}, {}
    for h, p in both:
        first = jnp.concatenate(ws[h, p], axis=1)
        second = jnp.concatenate(fs[h, p], axis=1)
        wn2 = jnp.concatenate([wn[h], wn[h]], axis=1)
        fn2 = jnp.concatenate([fn[h], fn[h]], axis=1)
        upper[h, p] = nt(first, fn2 if p == 0 else fn2[rows:])
        lower[h, p] = nt(second, wn2[:rows] if p == 0 else wn2)
    pairs, reads = {}, {}
    for h, p in both:
        if p == 0:
            own = jnp.where(before, lower[h, p], jnp.where(diagonal, 0.0, upper[h, p][:, :rows]))
            pairs[h, p] = jnp.concatenate([own, upper[h, p][:, rows:]], axis=1).astype(bf16)
            masked = jnp.concatenate(
                [jnp.where(seen_t, score_t[h, p][:, :half], 0.0), score_t[h, p][:, half:]], axis=1
            )
            reads[h, p] = nn(masked.astype(bf16), query[h])
        else:
            own = jnp.where(before, lower[h, p][:, rows:], jnp.where(diagonal, 0.0, upper[h, p]))
            pairs[h, p] = jnp.concatenate([lower[h, p][:, :rows], own], axis=1).astype(bf16)
            reads[h, p] = nn(jnp.where(seen_t, score_t[h, p], 0.0).astype(bf16), query[h][half:])
    for h in heads:
        masked = jnp.concatenate([
            jnp.concatenate([jnp.where(seen, score[h][:half, :rows], 0.0), jnp.zeros((half, rows), f32)], axis=1),
            jnp.concatenate([score[h][half:, :rows], jnp.where(seen, score[h][half:, rows:], 0.0)], axis=1),
        ], axis=0).astype(bf16)
        dq = nt(do_ref[h], state[h]) - nn(masked, all_keys[h])
        dq_ref[:, h * WIDTH : (h + 1) * WIDTH] = (dq * SCALE).astype(bf16)
    dk = {
        (h, p): nt(fs[h, p][0], state[h]) - reads[h, p] * SCALE - nt(ws[h, p][0], after[h]) - nn(pairs[h, p], all_keys[h])
        for h, p in both
    }
    units = {c: keys[c].astype(f32) * norm[c] for c in both}
    along = {c: jnp.sum(units[c] * dk[c], axis=1, keepdims=True) for c in both}
    for h, p in both:
        put(dk_ref, h, p, (norm[h, p] * (dk[h, p] - units[h, p] * along[h, p])).astype(bf16))


def whole(shape):
    return pl.BlockSpec(shape, lambda *unused: (0,) * len(shape))


def run(kernel, name, args, in_specs, outs, out_specs, grid=(1,), scratch=(), cost=None, vmem=16):
    return pl.pallas_call(
        kernel,
        name=name,
        grid=grid,
        in_specs=in_specs,
        out_specs=out_specs,
        scratch_shapes=list(scratch),
        out_shape=[jax.ShapeDtypeStruct(shape, dtype) for shape, dtype in outs],
        compiler_params=pltpu.CompilerParams(vmem_limit_bytes=vmem * 2**20),
        cost_estimate=cost,
    )(*args)


def small(kernel, name, args, outs, scratch=()):
    return run(
        kernel, name, args,
        [whole(a.shape) for a in args],
        outs,
        [whole(shape) for shape, unused in outs],
        scratch=scratch,
    )


def shards(queries, key_input, value_input, beta_rates, out_grad, out_weight):
    tokens = queries.shape[0]
    heads = queries.shape[1] // WIDTH
    rows = 2 * tokens
    model = out_weight.shape[1]
    key_input, value_input, queries, out_weight, beta_rates = (
        pltpu.with_memory_space_constraint(a, pltpu.HBM)
        for a in (key_input, value_input, queries, out_weight, beta_rates)
    )

    def move(value, target):
        return lax.ppermute(value, "ctx", [(i, target(i)) for i in range(32)])

    def other_core(i):
        return i ^ 1

    def along_x(by):
        return lambda i: (i // 8) * 8 + ((i // 2 + by) % HALF) * 2 + i % 2

    def along_y(by):
        return lambda i: (i + 8 * by) % 32

    def kv_spec(count):
        return pl.BlockSpec((2, tokens, count * WIDTH), lambda s: (0, 0, s))

    def q_spec(count):
        return pl.BlockSpec((tokens, count * WIDTH), lambda s: (0, s))

    def b_spec(count):
        return pl.BlockSpec((count, 2, tokens), lambda s: (s, 0, 0))

    def by_step(count, *shape):
        return pl.BlockSpec((count,) + shape, lambda s: (s,) + (0,) * len(shape))

    gathered = [out_grad] + [
        lax.ppermute(out_grad, "head", [(i, (i + by) % HALF) for i in range(HALF)]) for by in (1, 3, 2)
    ]
    gathered = [gathered[0], gathered[1], gathered[3], gathered[2]]
    tile = (2, tokens, tokens)
    send, keep, nh, nl, yh, yl, z, sh, sl, rh, rl, ph, plow, near = run(
        maps_kernel, "maps", (key_input, value_input, queries, beta_rates, out_weight),
        [kv_spec(MAPS_HEADS), kv_spec(MAPS_HEADS), q_spec(MAPS_HEADS), b_spec(MAPS_HEADS), pl.BlockSpec(memory_space=pl.ANY)],
        [((HALF, WIDTH, 2 * WIDTH), bf16)] * 2 + [((heads,) + tile, bf16)] * 4 + [((heads,) + tile, f32)]
        + [((heads,) + tile, bf16)] * 2 + [((heads, tokens, WIDTH), bf16)] * 2 + [((heads,) + tile, bf16)] * 2 + [(out_weight.shape, bf16)],
        [whole((HALF, WIDTH, 2 * WIDTH))] * 2 + [by_step(MAPS_HEADS, *tile)] * 7
        + [by_step(MAPS_HEADS, tokens, WIDTH)] * 2 + [by_step(MAPS_HEADS, *tile)] * 2 + [pl.BlockSpec(memory_space=pltpu.VMEM)],
        grid=(heads // MAPS_HEADS,),
        scratch=[pltpu.SemaphoreType.DMA],
        vmem=30,
        cost=pl.CostEstimate(flops=14_000_000_000, transcendentals=0, bytes_accessed=8_000_000),
    )
    got = move(send, other_core)
    gsend, gkeep, grad = run(
        local_grad_kernel, "local_grad", (*gathered, near, rh, rl),
        [
            *[whole(out_grad.shape)] * HALF,
            pl.BlockSpec(memory_space=pltpu.VMEM),
            *[by_step(LOCAL_HEADS, tokens, WIDTH)] * 2,
        ],
        [((HALF, WIDTH, WIDTH), bf16)] * 2 + [((heads, tokens, WIDTH), bf16)],
        [whole((HALF, WIDTH, WIDTH))] * 2 + [by_step(LOCAL_HEADS, tokens, WIDTH)],
        grid=(heads // LOCAL_HEADS,),
        scratch=[pltpu.VMEM((tokens, model), bf16)],
        vmem=24,
        cost=pl.CostEstimate(flops=2_000_000_000, transcendentals=0, bytes_accessed=10_000_000),
    )
    ggot = move(gsend, other_core)
    map_shape = ((WIDTH, 3 * WIDTH), bf16)
    chip = small(pair_kernel, "pair", (keep, got, gkeep, ggot), [map_shape] * HALF)
    chip = list(chip)
    chip[0], grad = lax.optimization_barrier((chip[0], grad))
    (reached,) = run(
        prep_kernel, "prep", (key_input, beta_rates, grad, nh, nl, sh, sl),
        [
            kv_spec(PREP_HEADS), b_spec(PREP_HEADS), by_step(PREP_HEADS, tokens, WIDTH),
            *[by_step(PREP_HEADS, *tile)] * 4,
        ],
        [((heads,) + tile, f32)],
        [by_step(PREP_HEADS, *tile)],
        grid=(heads // PREP_HEADS,),
        vmem=24,
        cost=pl.CostEstimate(flops=4_000_000_000, transcendentals=0, bytes_accessed=6_000_000),
    )
    chip = [chip[0]] + [move(chip[by], along_x(by)) for by in range(1, HALF)]
    chip[0], reached = lax.optimization_barrier((chip[0], reached))
    slots = pltpu.VMEM((HALF, WIDTH, 3 * WIDTH), bf16)
    (line,) = small(row_kernel, "line", chip, [map_shape], [slots])
    lines = [line] + [move(line, along_y(by)) for by in range(1, HALF)]
    ends_shape = ((WIDTH, 2 * WIDTH), bf16)
    ends_slots = pltpu.VMEM((HALF, WIDTH, 2 * WIDTH), bf16)
    ends = small(expand_kernel, "expand", chip + lines, [ends_shape] * HALF, [slots, slots, ends_slots])
    ends = [ends[0]] + [move(ends[by], along_x(by)) for by in range(1, HALF)]
    own, passed = small(
        down_kernel, "down", ends + [keep, got, gkeep, ggot],
        [((HALF, WIDTH, 2 * WIDTH), bf16)] * 2, [ends_slots],
    )
    taken = move(passed, other_core)
    return tuple(run(
        grads_kernel, "grads",
        (key_input, queries, beta_rates, grad, yh, yl, z, ph, plow, reached, own, taken),
        [
            kv_spec(GRADS_HEADS), q_spec(GRADS_HEADS), b_spec(GRADS_HEADS), by_step(GRADS_HEADS, tokens, WIDTH),
            *[by_step(GRADS_HEADS, *tile)] * 6,
            whole((HALF, WIDTH, 2 * WIDTH)), whole((HALF, WIDTH, 2 * WIDTH)),
        ],
        [
            (queries.shape, bf16), (key_input.shape, bf16), (value_input.shape, bf16), (beta_rates.shape, f32),
        ],
        [q_spec(GRADS_HEADS), kv_spec(GRADS_HEADS), kv_spec(GRADS_HEADS), b_spec(GRADS_HEADS)],
        grid=(heads // GRADS_HEADS,),
        vmem=24,
        cost=pl.CostEstimate(flops=8_000_000_000, transcendentals=0, bytes_accessed=14_000_000),
    ))


def solution(mesh):
    placed = (
        P("ctx", "head"),
        P(None, "ctx", "head"),
        P(None, "ctx", "head"),
        P("head", None, "ctx"),
        P(("ctx", "head"), None),
        P("head", None),
    )
    return jax.shard_map(
        shards,
        mesh=mesh,
        in_specs=placed,
        out_specs=(
            P("ctx", "head"),
            P(None, "ctx", "head"),
            P(None, "ctx", "head"),
            P("head", None, "ctx"),
        ),
        check_vma=False,
    )
```

```python
import functools

import jax
import jax.numpy as jnp
from jax import lax
from jax.experimental import pallas as pl
from jax.experimental.pallas import tpu as pltpu
from jax.sharding import PartitionSpec as P

WIDTH = 128
HALF = 4
MAPS_HEADS = 8
LOCAL_HEADS = 8
PREP_HEADS = 8
GRADS_HEADS = 8
SCALE = WIDTH ** (-0.5)
bf16 = jnp.bfloat16
f32 = jnp.float32


def dims(left, right):
    return (((left,), (right,)), ((), ()))


def nn(a, b):
    return lax.dot_general(a, b, dims(1, 0), preferred_element_type=f32)


def nt(a, b):
    return lax.dot_general(a, b, dims(1, 1), preferred_element_type=f32)


def tn(a, b):
    return lax.dot_general(a, b, dims(0, 0), preferred_element_type=f32)


def split(x):
    high = x.astype(bf16)
    return high, (x - high.astype(f32)).astype(bf16)


def iota(shape, dim):
    return lax.broadcasted_iota(jnp.int32, shape, dim)


def order(shape, dim):
    index = iota(shape, dim)
    tokens = shape[dim] // 2
    return jnp.where(index < tokens, 2 * index, 2 * (index - tokens) + 1)


def level_table(rows):
    left = order((rows, rows), 0)
    right = order((rows, rows), 1)
    differ = left ^ right
    level = jnp.zeros((rows, rows), jnp.int32)
    for bit in range(1, (rows - 1).bit_length()):
        level = level + (differ >= (1 << bit)).astype(jnp.int32)
    return jnp.where(left > right, level, -1)


def eye_mask(rows):
    return iota((rows, rows), 0) == iota((rows, rows), 1)


def column(row, diagonal):
    return jnp.sum(jnp.where(diagonal, row, 0.0), axis=1, keepdims=True)


def inverse_norms(keys):
    wide = keys.astype(f32)
    return lax.rsqrt(jnp.sum(wide * wide, axis=1, keepdims=True) + 1e-06)


def pick(ref, head, part):
    lanes = slice(head * WIDTH, (head + 1) * WIDTH)
    half = ref.shape[1] // 2
    span = slice(part * half, (part + 1) * half)
    return jnp.concatenate([ref[0, span, lanes], ref[1, span, lanes]], axis=0)


def put(ref, head, part, value):
    lanes = slice(head * WIDTH, (head + 1) * WIDTH)
    half = ref.shape[1] // 2
    span = slice(part * half, (part + 1) * half)
    ref[0, span, lanes] = value[:half]
    ref[1, span, lanes] = value[half:]


def rate_row(ref, head, part):
    half = ref.shape[2] // 2
    span = slice(part * half, (part + 1) * half)
    return jnp.concatenate([ref[head, 0:1, span], ref[head, 1:2, span]], axis=1)


def here():
    me = lax.axis_index("ctx")
    return me % 2, lax.rem(me // 2, HALF), me // (2 * HALF)


def maps_kernel(
    k_ref, v_ref, q_ref, b_ref, w_ref, send_ref, keep_ref, nh_ref, nl_ref, yh_ref, yl_ref, z_ref, sh_ref, sl_ref,
    rh_ref, rl_ref, ph_ref, pl_ref, near_ref, near_sem,
):
    fetch = pltpu.make_async_copy(w_ref, near_ref, near_sem)
    fetch.start()
    rows = k_ref.shape[1]
    level_of = level_table(rows)
    diagonal = eye_mask(rows)
    heads = range(MAPS_HEADS)
    chains = [(h, part) for h in heads for part in range(2)]
    every = range(len(chains))
    keys = [pick(k_ref, h, part) for h, part in chains]
    rates = [rate_row(b_ref, h, part) for h, part in chains]
    rate_cols = [column(r, diagonal) for r in rates]
    norms = [inverse_norms(k) for k in keys]
    grams = []
    for i in every:
        raw = nt(keys[i], keys[i])
        norm_row = lax.rsqrt(jnp.sum(jnp.where(diagonal, raw, 0.0), axis=0, keepdims=True) + 1e-06)
        grams.append(jnp.where(level_of >= 0, raw * norms[i] * norm_row, 0.0))
    half = rows // 2
    seen = order((rows, half), 0) < 2 * (iota((rows, half), 1) + 1)
    scores = {}
    for i, (h, part) in enumerate(chains):
        query = q_ref[:, h * WIDTH : (h + 1) * WIDTH]
        score = nt(keys[i], query) * (norms[i] * SCALE)
        if part == 0:
            score = jnp.concatenate([jnp.where(seen, score[:, :half], 0.0), score[:, half:]], axis=1)
        else:
            score = jnp.concatenate([jnp.zeros((rows, half), f32), jnp.where(seen, score[:, half:], 0.0)], axis=1)
        scores[h, part] = split(score)
        sh_ref[h, part], sl_ref[h, part] = scores[h, part]
    core = list(grams)
    for level in range((rows - 1).bit_length()):
        joins = [jnp.where(level_of == level, core[i] * rates[i], 0.0).astype(bf16) for i in every]
        core = [core[i] - nn(joins[i], core[i].astype(bf16)) for i in every]
    core_high = [c.astype(bf16) for c in core]
    residual = []
    for i in every:
        high, low = split(grams[i] * rates[i])
        residual.append(grams[i] - core_high[i].astype(f32) - nn(high, core_high[i]) - nn(low, core_high[i]))
    core_low = [
        (residual[i] - nn(core_high[i], (rate_cols[i] * residual[i]).astype(bf16))).astype(bf16) for i in every
    ]
    for i, (h, part) in enumerate(chains):
        nh_ref[h, part] = core_high[i]
        nl_ref[h, part] = core_low[i]

    mapped = [None for h in heads]
    weighted, adjoint = {}, {}
    for part in range(2):
        now = [2 * h + part for h in heads]
        late = [2 * h + 1 - part for h in heads]
        both = [
            jnp.concatenate([keys[i].astype(f32) * norms[i], pick(v_ref, h, part).astype(f32)], axis=1)
            for h, i in enumerate(now)
        ]
        ahead = [keys[i].astype(f32) * norms[i] for i in late]
        if part:
            pieces = [split(m) for m in mapped]
            both = [
                both[h] - norms[i] * (nn(keys[i], pieces[h][0]) + nn(keys[i], pieces[h][1])) for h, i in enumerate(now)
            ]
            pieces = [split(adjoint[h] * (rate_cols[i + 1] * norms[i + 1])) for h, i in enumerate(late)]
            passed = [tn(keys[i + 1], pieces[h][0]) + tn(keys[i + 1], pieces[h][1]) for h, i in enumerate(late)]
            pieces = [split(p) for p in passed]
            ahead = [
                ahead[h] - norms[i] * (nn(keys[i], pieces[h][0]) + nn(keys[i], pieces[h][1]))
                for h, i in enumerate(late)
            ]
        pieces = [split(both[h] * rate_cols[i]) for h, i in enumerate(now)]
        solved = [
            both[h] - nn(core_high[i], pieces[h][0]) - nn(core_low[i], pieces[h][0]) - nn(core_high[i], pieces[h][1])
            for h, i in enumerate(now)
        ]
        pieces = [split(ahead[h] * rate_cols[i]) for h, i in enumerate(late)]
        adjoint = [
            ahead[h] - tn(core_high[i], pieces[h][0]) - tn(core_low[i], pieces[h][0]) - tn(core_high[i], pieces[h][1])
            for h, i in enumerate(late)
        ]
        for h, i in enumerate(now):
            yh_ref[h, part], yl_ref[h, part] = split(solved[h][:, :WIDTH])
            z_ref[h, part] = solved[h][:, WIDTH:]
            weighted[h, part] = split(solved[h][:, :WIDTH] * rate_cols[i])
        pieces = [split(solved[h] * (rate_cols[i] * norms[i])) for h, i in enumerate(now)]
        found = [tn(keys[i], pieces[h][0]) + tn(keys[i], pieces[h][1]) for h, i in enumerate(now)]
        mapped = [found[h] if part == 0 else mapped[h] + found[h] for h in heads]
        for h in heads:
            ph_ref[h, 1 - part], pl_ref[h, 1 - part] = split(adjoint[h])
    place_halves(send_ref, keep_ref, mapped)

    stacked = [
        [jnp.concatenate([pair[h, 0][k], pair[h, 1][k]], axis=0) for pair in (scores, weighted) for k in range(2)]
        for h in heads
    ]
    taken = [tn(sh, wh) + tn(sl, wh) + tn(sh, wl) for sh, sl, wh, wl in stacked]
    for h in heads:
        rh_ref[h], rl_ref[h] = split(q_ref[:, h * WIDTH : (h + 1) * WIDTH].astype(f32) * SCALE - taken[h])
    fetch.wait()


def place_halves(send_ref, keep_ref, values):
    first = here()[0] == 0
    for slot in range(HALF):
        low, high = values[slot], values[HALF + slot]
        keep_ref[slot] = jnp.where(first, low, high).astype(bf16)
        send_ref[slot] = jnp.where(first, high, low).astype(bf16)


def local_grad_kernel(o0, o1, o2, o3, w_ref, rh_ref, rl_ref, send_ref, keep_ref, do_ref, og_ref):
    part = o0.shape[0]
    for shift, ref in enumerate((o0, o1, o2, o3)):
        where = pl.multiple_of(lax.rem(lax.axis_index("head") + HALF - shift, HALF) * part, part)
        og_ref[pl.ds(where, part), :] = ref[...]
    grads = nt(og_ref[...], w_ref[...]).astype(bf16)
    found = []
    for h in range(LOCAL_HEADS):
        grad = grads[:, h * WIDTH : (h + 1) * WIDTH]
        do_ref[h] = grad
        found.append(tn(rh_ref[h], grad) + tn(rl_ref[h], grad))
    place_halves(send_ref, keep_ref, found)


def prep_kernel(k_ref, b_ref, do_ref, nh_ref, nl_ref, sh_ref, sl_ref, u_ref):
    heads = range(PREP_HEADS)
    rows = k_ref.shape[1]
    diagonal = eye_mask(rows)
    reached = {
        (h, part): nn(sh_ref[h, part], do_ref[h]) + nn(sl_ref[h, part], do_ref[h]) for part in (1, 0) for h in heads
    }
    keys = {(h, part): pick(k_ref, h, part) for part in (1, 0) for h in heads}
    norms = {c: inverse_norms(keys[c]) for c in keys}
    rates = {(h, part): column(rate_row(b_ref, h, part), diagonal) for part in (1, 0) for h in heads}
    solved = [None]*8
    for part in (1, 0):
        ahead = [reached[h, part] for h in heads]
        if part == 0:
            pieces = [split(solved[h] * (rates[h, 1] * norms[h, 1])) for h in heads]
            passed = [tn(keys[h, 1], pieces[h][0]) + tn(keys[h, 1], pieces[h][1]) for h in heads]
            pieces = [split(p) for p in passed]
            ahead = [
                ahead[h] - norms[h, 0] * (nn(keys[h, 0], pieces[h][0]) + nn(keys[h, 0], pieces[h][1])) for h in heads
            ]
        pieces = [split(ahead[h] * rates[h, part]) for h in heads]
        solved = [
            ahead[h] - tn(nh_ref[h, part], pieces[h][0]) - tn(nl_ref[h, part], pieces[h][0])
            - tn(nh_ref[h, part], pieces[h][1])
            for h in heads
        ]
        for h in heads:
            u_ref[h, part] = solved[h]


def pair_kernel(keep_ref, got_ref, gkeep_ref, ggot_ref, *outs):
    core, spot, unused = here()
    for shift in range(HALF):
        slot = lax.rem(spot + shift, HALF)
        mine, other = keep_ref[slot].astype(f32), got_ref[slot].astype(f32)
        first = jnp.where(core == 0, mine, other)
        second = jnp.where(core == 0, other, mine)
        mine, other = gkeep_ref[slot].astype(f32), ggot_ref[slot].astype(f32)
        gfirst = jnp.where(core == 0, mine, other)
        gsecond = jnp.where(core == 0, other, mine)
        joined = first + second - nn(second[:, :WIDTH].astype(bf16), first.astype(bf16))
        gjoined = gfirst + gsecond - tn(first[:, :WIDTH].astype(bf16), gsecond.astype(bf16))
        outs[shift][:, : 2 * WIDTH] = joined.astype(bf16)
        outs[shift][:, 2 * WIDTH :] = gjoined.astype(bf16)


def join(first, second):
    forward = first[:, : 2 * WIDTH] + second[:, : 2 * WIDTH]
    forward = forward - nn(second[:, :WIDTH].astype(bf16), first[:, : 2 * WIDTH].astype(bf16))
    backward = first[:, 2 * WIDTH :] + second[:, 2 * WIDTH :]
    backward = backward - tn(first[:, :WIDTH].astype(bf16), second[:, 2 * WIDTH :].astype(bf16))
    return jnp.concatenate([forward, backward], axis=1)


def gather_slots(slots, refs, spot):
    for shift in range(HALF):
        slots[lax.rem(spot + HALF - shift, HALF)] = refs[shift][...]


def row_kernel(a_ref, b_ref, c_ref, d_ref, out_ref, slots):
    gather_slots(slots, (a_ref, b_ref, c_ref, d_ref), here()[1])
    maps = [slots[i].astype(f32) for i in range(HALF)]
    out_ref[...] = join(join(maps[0], maps[1]), join(maps[2], maps[3])).astype(bf16)


def advance(block, state):
    high, low = split(state)
    moved = nn(block[:, :WIDTH], jnp.concatenate([high, low], axis=1))
    return state - moved[:, :WIDTH] - moved[:, WIDTH:] + block[:, WIDTH : 2 * WIDTH].astype(f32)


def retreat(block, grad):
    high, low = split(grad)
    moved = tn(block[:, :WIDTH], jnp.concatenate([high, low], axis=1))
    return grad - moved[:, :WIDTH] - moved[:, WIDTH:] + block[:, 2 * WIDTH :].astype(f32)


def expand_kernel(a_ref, b_ref, c_ref, d_ref, e_ref, f_ref, g_ref, h_ref, o0, o1, o2, o3, chips, lines, found):
    unused, spot, line = here()
    gather_slots(chips, (a_ref, b_ref, c_ref, d_ref), spot)
    gather_slots(lines, (e_ref, f_ref, g_ref, h_ref), line)
    state = jnp.where(line > 0, lines[0, :, WIDTH : 2 * WIDTH].astype(f32), 0.0)
    grad = jnp.where(line < HALF - 1, lines[HALF - 1, :, 2 * WIDTH :].astype(f32), 0.0)
    for i in range(1, HALF - 1):
        state = jnp.where(i < line, advance(lines[i], state), state)
        back = HALF - 1 - i
        grad = jnp.where(back > line, retreat(lines[back], grad), grad)
    for i in range(HALF):
        found[i, :, :WIDTH] = state.astype(bf16)
        back = HALF - 1 - i
        found[back, :, WIDTH:] = grad.astype(bf16)
        if i < HALF - 1:
            state = advance(chips[i], state)
            grad = retreat(chips[back], grad)
    for shift, out in enumerate((o0, o1, o2, o3)):
        out[...] = found[lax.rem(spot + shift, HALF)]


def down_kernel(a_ref, b_ref, c_ref, d_ref, keep_ref, got_ref, gkeep_ref, ggot_ref, own_ref, send_ref, slots):
    core, spot, unused = here()
    gather_slots(slots, (a_ref, b_ref, c_ref, d_ref), spot)
    for slot in range(HALF):
        state = slots[slot, :, :WIDTH]
        grad = slots[slot, :, WIDTH:]
        first = jnp.where(core == 0, keep_ref[slot].astype(f32), got_ref[slot].astype(f32))
        second = jnp.where(core == 0, got_ref[slot, :, :WIDTH].astype(f32), keep_ref[slot, :, :WIDTH].astype(f32))
        gsecond = jnp.where(core == 0, ggot_ref[slot].astype(f32), gkeep_ref[slot].astype(f32))
        middle = state.astype(f32) - nn(first[:, :WIDTH].astype(bf16), state) + first[:, WIDTH:]
        gmiddle = grad.astype(f32) - tn(second.astype(bf16), grad) + gsecond
        early = jnp.concatenate([state.astype(f32), gmiddle], axis=1)
        late = jnp.concatenate([middle, grad.astype(f32)], axis=1)
        own_ref[slot] = jnp.where(core == 0, early, late).astype(bf16)
        send_ref[slot] = jnp.where(core == 0, late, early).astype(bf16)


def grads_kernel(
    k_ref, q_ref, b_ref, do_ref, yh_ref, yl_ref, z_ref, ph_ref, pl_ref, u_ref, own_ref, got_ref,
    dq_ref, dk_ref, dv_ref, db_ref,
):
    step = pl.program_id(0)
    core = here()[0]
    heads = range(GRADS_HEADS)
    parts = range(2)
    both = [(h, p) for h in heads for p in parts]
    tokens = q_ref.shape[0]
    half = tokens // 2
    rows = 2 * half
    diagonal = eye_mask(rows)
    before = order((rows, rows), 1) < order((rows, rows), 0)
    seen = order((half, rows), 1) < 2 * (iota((half, rows), 0) + 1)
    seen_t = order((rows, half), 0) < 2 * (iota((rows, half), 1) + 1)
    state, after = [], []
    for h in heads:
        head = step * GRADS_HEADS + h
        slot = lax.rem(head, HALF)
        mine = head // HALF == core
        ends = jnp.where(mine, own_ref[slot].astype(f32), got_ref[slot].astype(f32)).astype(bf16)
        state.append(ends[:, :WIDTH])
        after.append(ends[:, WIDTH:])
    keys = {(h, p): pick(k_ref, h, p) for h, p in both}
    rate = {(h, p): column(rate_row(b_ref, h, p), diagonal) for h, p in both}
    norm = {c: inverse_norms(keys[c]) for c in both}
    query = [q_ref[:, h * WIDTH : (h + 1) * WIDTH] for h in heads]

    errors, back = {}, {}
    for h, p in both:
        errors[h, p] = nn(yh_ref[h, p], state[h]) + nn(yl_ref[h, p], state[h]) - z_ref[h, p]
        back[h, p] = -u_ref[h, p] - nn(ph_ref[h, p], after[h]) - nn(pl_ref[h, p], after[h])
    weighted = {c: errors[c] * rate[c] for c in both}
    scaled = {c: back[c] * rate[c] for c in both}
    d_rate = {c: jnp.sum(errors[c] * back[c], axis=1, keepdims=True) for c in both}
    d_rate = {c: jnp.sum(jnp.where(diagonal, d_rate[c], 0.0), axis=0, keepdims=True) for c in both}
    for h, p in both:
        db_ref[h, 0:1, p * half : (p + 1) * half] = d_rate[h, p][:, :half]
        db_ref[h, 1:2, p * half : (p + 1) * half] = d_rate[h, p][:, half:]
        put(dv_ref, h, p, (-scaled[h, p]).astype(bf16))
    ws = {c: split(weighted[c]) for c in both}
    fs = {c: split(scaled[c]) for c in both}
    wn = [jnp.concatenate([(weighted[h, p] * norm[h, p]).astype(bf16) for p in parts], axis=0) for h in heads]
    fn = [jnp.concatenate([(scaled[h, p] * norm[h, p]).astype(bf16) for p in parts], axis=0) for h in heads]
    all_keys = [jnp.concatenate([keys[h, p] for p in parts], axis=0) for h in heads]

    score = [nt(do_ref[h], wn[h]) for h in heads]
    score_t = {(h, p): nt(ws[h, p][0], do_ref[h] if p == 0 else do_ref[h, half:]) for h, p in both}
    lower, upper = {}, {}
    for h, p in both:
        first = jnp.concatenate(ws[h, p], axis=1)
        second = jnp.concatenate(fs[h, p], axis=1)
        wn2 = jnp.concatenate([wn[h], wn[h]], axis=1)
        fn2 = jnp.concatenate([fn[h], fn[h]], axis=1)
        upper[h, p] = nt(first, fn2 if p == 0 else fn2[rows:])
        lower[h, p] = nt(second, wn2[:rows] if p == 0 else wn2)
    pairs, reads = {}, {}
    for h, p in both:
        if p == 0:
            own = jnp.where(before, lower[h, p], jnp.where(diagonal, 0.0, upper[h, p][:, :rows]))
            pairs[h, p] = jnp.concatenate([own, upper[h, p][:, rows:]], axis=1).astype(bf16)
            masked = jnp.concatenate(
                [jnp.where(seen_t, score_t[h, p][:, :half], 0.0), score_t[h, p][:, half:]], axis=1
            )
            reads[h, p] = nn(masked.astype(bf16), query[h])
        else:
            own = jnp.where(before, lower[h, p][:, rows:], jnp.where(diagonal, 0.0, upper[h, p]))
            pairs[h, p] = jnp.concatenate([lower[h, p][:, :rows], own], axis=1).astype(bf16)
            reads[h, p] = nn(jnp.where(seen_t, score_t[h, p], 0.0).astype(bf16), query[h][half:])
    for h in heads:
        masked = jnp.concatenate([
            jnp.concatenate([jnp.where(seen, score[h][:half, :rows], 0.0), jnp.zeros((half, rows), f32)], axis=1),
            jnp.concatenate([score[h][half:, :rows], jnp.where(seen, score[h][half:, rows:], 0.0)], axis=1),
        ], axis=0).astype(bf16)
        dq = nt(do_ref[h], state[h]) - nn(masked, all_keys[h])
        dq_ref[:, h * WIDTH : (h + 1) * WIDTH] = (dq * SCALE).astype(bf16)
    dk = {
        (h, p): nt(fs[h, p][0], state[h]) - reads[h, p] * SCALE - nt(ws[h, p][0], after[h]) - nn(pairs[h, p], all_keys[h])
        for h, p in both
    }
    units = {c: keys[c].astype(f32) * norm[c] for c in both}
    along = {c: jnp.sum(units[c] * dk[c], axis=1, keepdims=True) for c in both}
    for h, p in both:
        put(dk_ref, h, p, (norm[h, p] * (dk[h, p] - units[h, p] * along[h, p])).astype(bf16))


def whole(shape):
    return pl.BlockSpec(shape, lambda *unused: (0,) * len(shape))


def run(kernel, name, args, in_specs, outs, out_specs, grid=(1,), scratch=(), cost=None, vmem=16):
    return pl.pallas_call(
        kernel,
        name=name,
        grid=grid,
        in_specs=in_specs,
        out_specs=out_specs,
        scratch_shapes=list(scratch),
        out_shape=[jax.ShapeDtypeStruct(shape, dtype) for shape, dtype in outs],
        compiler_params=pltpu.CompilerParams(vmem_limit_bytes=vmem * 2**20),
        cost_estimate=cost,
    )(*args)


def small(kernel, name, args, outs, scratch=()):
    return run(
        kernel, name, args,
        [whole(a.shape) for a in args],
        outs,
        [whole(shape) for shape, unused in outs],
        scratch=scratch,
    )


def shards(queries, key_input, value_input, beta_rates, out_grad, out_weight):
    tokens = queries.shape[0]
    heads = queries.shape[1] // WIDTH
    rows = 2 * tokens
    model = out_weight.shape[1]
    near_keys, near_queries, near_rates = key_input, queries, beta_rates
    key_input, value_input, queries, out_weight, beta_rates = (
        pltpu.with_memory_space_constraint(a, pltpu.HBM)
        for a in (key_input, value_input, queries, out_weight, beta_rates)
    )

    def move(value, target):
        return lax.ppermute(value, "ctx", [(i, target(i)) for i in range(32)])

    def other_core(i):
        return i ^ 1

    def along_x(by):
        return lambda i: (i // 8) * 8 + ((i // 2 + by) % HALF) * 2 + i % 2

    def along_y(by):
        return lambda i: (i + 8 * by) % 32

    def kv_spec(count):
        return pl.BlockSpec((2, tokens, count * WIDTH), lambda s: (0, 0, s))

    def q_spec(count):
        return pl.BlockSpec((tokens, count * WIDTH), lambda s: (0, s))

    def b_spec(count):
        return pl.BlockSpec((count, 2, tokens), lambda s: (s, 0, 0))

    def by_step(count, *shape):
        return pl.BlockSpec((count,) + shape, lambda s: (s,) + (0,) * len(shape))

    gathered = [out_grad] + [
        lax.ppermute(out_grad, "head", [(i, (i + by) % HALF) for i in range(HALF)]) for by in (1, 3, 2)
    ]
    gathered = [gathered[0], gathered[1], gathered[3], gathered[2]]
    tile = (2, tokens, tokens)
    send, keep, nh, nl, yh, yl, z, sh, sl, rh, rl, ph, plow, near = run(
        maps_kernel, "maps", (key_input, value_input, queries, beta_rates, out_weight),
        [kv_spec(MAPS_HEADS), kv_spec(MAPS_HEADS), q_spec(MAPS_HEADS), b_spec(MAPS_HEADS), pl.BlockSpec(memory_space=pl.ANY)],
        [((HALF, WIDTH, 2 * WIDTH), bf16)] * 2 + [((heads,) + tile, bf16)] * 4 + [((heads,) + tile, f32)]
        + [((heads,) + tile, bf16)] * 2 + [((heads, tokens, WIDTH), bf16)] * 2 + [((heads,) + tile, bf16)] * 2 + [(out_weight.shape, bf16)],
        [whole((HALF, WIDTH, 2 * WIDTH))] * 2 + [by_step(MAPS_HEADS, *tile)] * 7
        + [by_step(MAPS_HEADS, tokens, WIDTH)] * 2 + [by_step(MAPS_HEADS, *tile)] * 2 + [pl.BlockSpec(memory_space=pltpu.VMEM)],
        grid=(heads // MAPS_HEADS,),
        scratch=[pltpu.SemaphoreType.DMA],
        vmem=30,
        cost=pl.CostEstimate(flops=14_000_000_000, transcendentals=0, bytes_accessed=8_000_000),
    )
    got = move(send, other_core)
    gsend, gkeep, grad = run(
        local_grad_kernel, "local_grad", (*gathered, near, rh, rl),
        [
            *[whole(out_grad.shape)] * HALF,
            pl.BlockSpec(memory_space=pltpu.VMEM),
            *[by_step(LOCAL_HEADS, tokens, WIDTH)] * 2,
        ],
        [((HALF, WIDTH, WIDTH), bf16)] * 2 + [((heads, tokens, WIDTH), bf16)],
        [whole((HALF, WIDTH, WIDTH))] * 2 + [by_step(LOCAL_HEADS, tokens, WIDTH)],
        grid=(heads // LOCAL_HEADS,),
        scratch=[pltpu.VMEM((tokens, model), bf16)],
        vmem=24,
        cost=pl.CostEstimate(flops=2_000_000_000, transcendentals=0, bytes_accessed=10_000_000),
    )
    ggot = move(gsend, other_core)
    map_shape = ((WIDTH, 3 * WIDTH), bf16)
    chip = small(pair_kernel, "pair", (keep, got, gkeep, ggot), [map_shape] * HALF)
    chip = list(chip)
    chip[0], grad = lax.optimization_barrier((chip[0], grad))
    (reached,) = run(
        prep_kernel, "prep", (near_keys, near_rates, grad, nh, nl, sh, sl),
        [
            kv_spec(PREP_HEADS), b_spec(PREP_HEADS), by_step(PREP_HEADS, tokens, WIDTH),
            *[by_step(PREP_HEADS, *tile)] * 4,
        ],
        [((heads,) + tile, f32)],
        [by_step(PREP_HEADS, *tile)],
        grid=(heads // PREP_HEADS,),
        vmem=24,
        cost=pl.CostEstimate(flops=4_000_000_000, transcendentals=0, bytes_accessed=6_000_000),
    )
    chip = [chip[0]] + [move(chip[by], along_x(by)) for by in range(1, HALF)]
    chip[0], reached = lax.optimization_barrier((chip[0], reached))
    slots = pltpu.VMEM((HALF, WIDTH, 3 * WIDTH), bf16)
    (line,) = small(row_kernel, "line", chip, [map_shape], [slots])
    lines = [line] + [move(line, along_y(by)) for by in range(1, HALF)]
    ends_shape = ((WIDTH, 2 * WIDTH), bf16)
    ends_slots = pltpu.VMEM((HALF, WIDTH, 2 * WIDTH), bf16)
    ends = small(expand_kernel, "expand", chip + lines, [ends_shape] * HALF, [slots, slots, ends_slots])
    ends = [ends[0]] + [move(ends[by], along_x(by)) for by in range(1, HALF)]
    own, passed = small(
        down_kernel, "down", ends + [keep, got, gkeep, ggot],
        [((HALF, WIDTH, 2 * WIDTH), bf16)] * 2, [ends_slots],
    )
    taken = move(passed, other_core)
    return tuple(run(
        grads_kernel, "grads",
        (near_keys, near_queries, near_rates, grad, yh, yl, z, ph, plow, reached, own, taken),
        [
            kv_spec(GRADS_HEADS), q_spec(GRADS_HEADS), b_spec(GRADS_HEADS), by_step(GRADS_HEADS, tokens, WIDTH),
            *[by_step(GRADS_HEADS, *tile)] * 6,
            whole((HALF, WIDTH, 2 * WIDTH)), whole((HALF, WIDTH, 2 * WIDTH)),
        ],
        [
            (queries.shape, bf16), (key_input.shape, bf16), (value_input.shape, bf16), (beta_rates.shape, f32),
        ],
        [q_spec(GRADS_HEADS), kv_spec(GRADS_HEADS), kv_spec(GRADS_HEADS), b_spec(GRADS_HEADS)],
        grid=(heads // GRADS_HEADS,),
        vmem=24,
        cost=pl.CostEstimate(flops=8_000_000_000, transcendentals=0, bytes_accessed=14_000_000),
    ))


def solution(mesh):
    placed = (
        P("ctx", "head"),
        P(None, "ctx", "head"),
        P(None, "ctx", "head"),
        P("head", None, "ctx"),
        P(("ctx", "head"), None),
        P("head", None),
    )
    return jax.shard_map(
        shards,
        mesh=mesh,
        in_specs=placed,
        out_specs=(
            P("ctx", "head"),
            P(None, "ctx", "head"),
            P(None, "ctx", "head"),
            P("head", None, "ctx"),
        ),
        check_vma=False,
    )
```

```python
import functools

import jax
import jax.numpy as jnp
from jax import lax
from jax.experimental import pallas as pl
from jax.experimental.pallas import tpu as pltpu
from jax.sharding import PartitionSpec as P

WIDTH = 128
HALF = 4
MAPS_HEADS = 8
LOCAL_HEADS = 8
PREP_HEADS = 8
GRADS_HEADS = 8
SCALE = WIDTH ** (-0.5)
bf16 = jnp.bfloat16
f32 = jnp.float32


def dims(left, right):
    return (((left,), (right,)), ((), ()))


def nn(a, b):
    return lax.dot_general(a, b, dims(1, 0), preferred_element_type=f32)


def nt(a, b):
    return lax.dot_general(a, b, dims(1, 1), preferred_element_type=f32)


def tn(a, b):
    return lax.dot_general(a, b, dims(0, 0), preferred_element_type=f32)


def split(x):
    high = x.astype(bf16)
    return high, (x - high.astype(f32)).astype(bf16)


def iota(shape, dim):
    return lax.broadcasted_iota(jnp.int32, shape, dim)


def order(shape, dim):
    index = iota(shape, dim)
    tokens = shape[dim] // 2
    return jnp.where(index < tokens, 2 * index, 2 * (index - tokens) + 1)


def level_table(rows):
    left = order((rows, rows), 0)
    right = order((rows, rows), 1)
    differ = left ^ right
    level = jnp.zeros((rows, rows), jnp.int32)
    for bit in range(1, (rows - 1).bit_length()):
        level = level + (differ >= (1 << bit)).astype(jnp.int32)
    return jnp.where(left > right, level, -1)


def eye_mask(rows):
    return iota((rows, rows), 0) == iota((rows, rows), 1)


def column(row, diagonal):
    return jnp.sum(jnp.where(diagonal, row, 0.0), axis=1, keepdims=True)


def inverse_norms(keys):
    wide = keys.astype(f32)
    return lax.rsqrt(jnp.sum(wide * wide, axis=1, keepdims=True) + 1e-06)


def pick(ref, head, part):
    lanes = slice(head * WIDTH, (head + 1) * WIDTH)
    half = ref.shape[1] // 2
    span = slice(part * half, (part + 1) * half)
    return jnp.concatenate([ref[0, span, lanes], ref[1, span, lanes]], axis=0)


def put(ref, head, part, value):
    lanes = slice(head * WIDTH, (head + 1) * WIDTH)
    half = ref.shape[1] // 2
    span = slice(part * half, (part + 1) * half)
    ref[0, span, lanes] = value[:half]
    ref[1, span, lanes] = value[half:]


def rate_row(ref, head, part):
    half = ref.shape[2] // 2
    span = slice(part * half, (part + 1) * half)
    return jnp.concatenate([ref[head, 0:1, span], ref[head, 1:2, span]], axis=1)


def here():
    me = lax.axis_index("ctx")
    return me % 2, lax.rem(me // 2, HALF), me // (2 * HALF)


def maps_kernel(
    k_ref, v_ref, q_ref, b_ref, w_ref, send_ref, keep_ref, nh_ref, nl_ref, yh_ref, yl_ref, z_ref, sh_ref, sl_ref,
    rh_ref, rl_ref, ph_ref, pl_ref, near_ref, near_sem,
):
    fetch = pltpu.make_async_copy(w_ref, near_ref, near_sem)
    fetch.start()
    rows = k_ref.shape[1]
    level_of = level_table(rows)
    diagonal = eye_mask(rows)
    heads = range(MAPS_HEADS)
    chains = [(h, part) for h in heads for part in range(2)]
    every = range(len(chains))
    keys = [pick(k_ref, h, part) for h, part in chains]
    rates = [rate_row(b_ref, h, part) for h, part in chains]
    rate_cols = [column(r, diagonal) for r in rates]
    norms = [inverse_norms(k) for k in keys]
    grams = []
    for i in every:
        raw = nt(keys[i], keys[i])
        norm_row = lax.rsqrt(jnp.sum(jnp.where(diagonal, raw, 0.0), axis=0, keepdims=True) + 1e-06)
        grams.append(jnp.where(level_of >= 0, raw * norms[i] * norm_row, 0.0))
    half = rows // 2
    seen = order((rows, half), 0) < 2 * (iota((rows, half), 1) + 1)
    scores = {}
    for i, (h, part) in enumerate(chains):
        query = q_ref[:, h * WIDTH : (h + 1) * WIDTH]
        score = nt(keys[i], query) * (norms[i] * SCALE)
        if part == 0:
            score = jnp.concatenate([jnp.where(seen, score[:, :half], 0.0), score[:, half:]], axis=1)
        else:
            score = jnp.concatenate([jnp.zeros((rows, half), f32), jnp.where(seen, score[:, half:], 0.0)], axis=1)
        scores[h, part] = split(score)
        sh_ref[h, part], sl_ref[h, part] = scores[h, part]
    core = list(grams)
    for level in range((rows - 1).bit_length()):
        joins = [jnp.where(level_of == level, core[i] * rates[i], 0.0).astype(bf16) for i in every]
        core = [core[i] - nn(joins[i], core[i].astype(bf16)) for i in every]
    core_high = [c.astype(bf16) for c in core]
    residual = []
    for i in every:
        high, low = split(grams[i] * rates[i])
        residual.append(grams[i] - core_high[i].astype(f32) - nn(high, core_high[i]) - nn(low, core_high[i]))
    core_low = [
        (residual[i] - nn(core_high[i], (rate_cols[i] * residual[i]).astype(bf16))).astype(bf16) for i in every
    ]
    for i, (h, part) in enumerate(chains):
        nh_ref[h, part] = core_high[i]
        nl_ref[h, part] = core_low[i]

    mapped = [None for h in heads]
    weighted, adjoint = {}, {}
    for part in range(2):
        now = [2 * h + part for h in heads]
        late = [2 * h + 1 - part for h in heads]
        both = [
            jnp.concatenate([keys[i].astype(f32) * norms[i], pick(v_ref, h, part).astype(f32)], axis=1)
            for h, i in enumerate(now)
        ]
        ahead = [keys[i].astype(f32) * norms[i] for i in late]
        if part:
            pieces = [split(m) for m in mapped]
            both = [
                both[h] - norms[i] * (nn(keys[i], pieces[h][0]) + nn(keys[i], pieces[h][1])) for h, i in enumerate(now)
            ]
            pieces = [split(adjoint[h] * (rate_cols[i + 1] * norms[i + 1])) for h, i in enumerate(late)]
            passed = [tn(keys[i + 1], pieces[h][0]) + tn(keys[i + 1], pieces[h][1]) for h, i in enumerate(late)]
            pieces = [split(p) for p in passed]
            ahead = [
                ahead[h] - norms[i] * (nn(keys[i], pieces[h][0]) + nn(keys[i], pieces[h][1]))
                for h, i in enumerate(late)
            ]
        pieces = [split(both[h] * rate_cols[i]) for h, i in enumerate(now)]
        solved = [
            both[h] - nn(core_high[i], pieces[h][0]) - nn(core_low[i], pieces[h][0]) - nn(core_high[i], pieces[h][1])
            for h, i in enumerate(now)
        ]
        pieces = [split(ahead[h] * rate_cols[i]) for h, i in enumerate(late)]
        adjoint = [
            ahead[h] - tn(core_high[i], pieces[h][0]) - tn(core_low[i], pieces[h][0]) - tn(core_high[i], pieces[h][1])
            for h, i in enumerate(late)
        ]
        for h, i in enumerate(now):
            yh_ref[h, part], yl_ref[h, part] = split(solved[h][:, :WIDTH])
            z_ref[h, part] = solved[h][:, WIDTH:]
            weighted[h, part] = split(solved[h][:, :WIDTH] * rate_cols[i])
        pieces = [split(solved[h] * (rate_cols[i] * norms[i])) for h, i in enumerate(now)]
        found = [tn(keys[i], pieces[h][0]) + tn(keys[i], pieces[h][1]) for h, i in enumerate(now)]
        mapped = [found[h] if part == 0 else mapped[h] + found[h] for h in heads]
        for h in heads:
            ph_ref[h, 1 - part], pl_ref[h, 1 - part] = split(adjoint[h])
    place_halves(send_ref, keep_ref, mapped)

    stacked = [
        [jnp.concatenate([pair[h, 0][k], pair[h, 1][k]], axis=0) for pair in (scores, weighted) for k in range(2)]
        for h in heads
    ]
    taken = [tn(sh, wh) + tn(sl, wh) + tn(sh, wl) for sh, sl, wh, wl in stacked]
    for h in heads:
        rh_ref[h], rl_ref[h] = split(q_ref[:, h * WIDTH : (h + 1) * WIDTH].astype(f32) * SCALE - taken[h])
    fetch.wait()


def place_halves(send_ref, keep_ref, values):
    first = here()[0] == 0
    for slot in range(HALF):
        low, high = values[slot], values[HALF + slot]
        keep_ref[slot] = jnp.where(first, low, high).astype(bf16)
        send_ref[slot] = jnp.where(first, high, low).astype(bf16)


def local_grad_kernel(o0, o1, o2, o3, w_ref, rh_ref, rl_ref, send_ref, keep_ref, do_ref, og_ref):
    part = o0.shape[0]
    for shift, ref in enumerate((o0, o1, o2, o3)):
        where = pl.multiple_of(lax.rem(lax.axis_index("head") + HALF - shift, HALF) * part, part)
        og_ref[pl.ds(where, part), :] = ref[...]
    grads = nt(og_ref[...], w_ref[...]).astype(bf16)
    found = []
    for h in range(LOCAL_HEADS):
        grad = grads[:, h * WIDTH : (h + 1) * WIDTH]
        do_ref[h] = grad
        found.append(tn(rh_ref[h], grad) + tn(rl_ref[h], grad))
    place_halves(send_ref, keep_ref, found)


def prep_kernel(k_ref, b_ref, do_ref, nh_ref, nl_ref, sh_ref, sl_ref, u_ref):
    heads = range(PREP_HEADS)
    rows = k_ref.shape[1]
    diagonal = eye_mask(rows)
    reached = {
        (h, part): nn(sh_ref[h, part], do_ref[h]) + nn(sl_ref[h, part], do_ref[h]) for part in (1, 0) for h in heads
    }
    keys = {(h, part): pick(k_ref, h, part) for part in (1, 0) for h in heads}
    norms = {c: inverse_norms(keys[c]) for c in keys}
    rates = {(h, part): column(rate_row(b_ref, h, part), diagonal) for part in (1, 0) for h in heads}
    solved = [None]*8
    for part in (1, 0):
        ahead = [reached[h, part] for h in heads]
        if part == 0:
            pieces = [split(solved[h] * (rates[h, 1] * norms[h, 1])) for h in heads]
            passed = [tn(keys[h, 1], pieces[h][0]) + tn(keys[h, 1], pieces[h][1]) for h in heads]
            pieces = [split(p) for p in passed]
            ahead = [
                ahead[h] - norms[h, 0] * (nn(keys[h, 0], pieces[h][0]) + nn(keys[h, 0], pieces[h][1])) for h in heads
            ]
        pieces = [split(ahead[h] * rates[h, part]) for h in heads]
        solved = [
            ahead[h] - tn(nh_ref[h, part], pieces[h][0]) - tn(nl_ref[h, part], pieces[h][0])
            - tn(nh_ref[h, part], pieces[h][1])
            for h in heads
        ]
        for h in heads:
            u_ref[h, part] = solved[h]


def pair_kernel(keep_ref, got_ref, gkeep_ref, ggot_ref, *outs):
    core, spot, unused = here()
    for shift in range(HALF):
        slot = lax.rem(spot + shift, HALF)
        mine, other = keep_ref[slot].astype(f32), got_ref[slot].astype(f32)
        first = jnp.where(core == 0, mine, other)
        second = jnp.where(core == 0, other, mine)
        mine, other = gkeep_ref[slot].astype(f32), ggot_ref[slot].astype(f32)
        gfirst = jnp.where(core == 0, mine, other)
        gsecond = jnp.where(core == 0, other, mine)
        joined = first + second - nn(second[:, :WIDTH].astype(bf16), first.astype(bf16))
        gjoined = gfirst + gsecond - tn(first[:, :WIDTH].astype(bf16), gsecond.astype(bf16))
        outs[shift][:, : 2 * WIDTH] = joined.astype(bf16)
        outs[shift][:, 2 * WIDTH :] = gjoined.astype(bf16)


def join(first, second):
    forward = first[:, : 2 * WIDTH] + second[:, : 2 * WIDTH]
    forward = forward - nn(second[:, :WIDTH].astype(bf16), first[:, : 2 * WIDTH].astype(bf16))
    backward = first[:, 2 * WIDTH :] + second[:, 2 * WIDTH :]
    backward = backward - tn(first[:, :WIDTH].astype(bf16), second[:, 2 * WIDTH :].astype(bf16))
    return jnp.concatenate([forward, backward], axis=1)


def gather_slots(slots, refs, spot):
    for shift in range(HALF):
        slots[lax.rem(spot + HALF - shift, HALF)] = refs[shift][...]


def row_kernel(a_ref, b_ref, c_ref, d_ref, o1, o2, o3, slots):
    gather_slots(slots, (a_ref, b_ref, c_ref, d_ref), here()[1])
    maps = [slots[i].astype(f32) for i in range(HALF)]
    joined = join(join(maps[0], maps[1]), join(maps[2], maps[3]))
    for shift, out in enumerate((o1, o2, o3)):
        later = here()[2] + shift + 1 < HALF
        out[:, :WIDTH] = joined[:, :WIDTH].astype(bf16)
        out[:, WIDTH:] = jnp.where(later, joined[:, WIDTH : 2 * WIDTH], joined[:, 2 * WIDTH :]).astype(bf16)


def advance(block, state):
    high, low = split(state)
    moved = nn(block[:, :WIDTH], jnp.concatenate([high, low], axis=1))
    return state - moved[:, :WIDTH] - moved[:, WIDTH:] + block[:, WIDTH : 2 * WIDTH].astype(f32)


def retreat(block, grad):
    high, low = split(grad)
    moved = tn(block[:, :WIDTH], jnp.concatenate([high, low], axis=1))
    return grad - moved[:, :WIDTH] - moved[:, WIDTH:] + block[:, block.shape[1] - WIDTH :].astype(f32)


def expand_kernel(a_ref, b_ref, c_ref, d_ref, f_ref, g_ref, h_ref, o0, o1, o2, o3, chips, lines, found):
    unused, spot, line = here()
    gather_slots(chips, (a_ref, b_ref, c_ref, d_ref), spot)
    for shift, ref in enumerate((f_ref, g_ref, h_ref)):
        lines[lax.rem(line + HALF - 1 - shift, HALF)] = ref[...]
    lines[line] = jnp.zeros((WIDTH, 2 * WIDTH), bf16)
    state = jnp.where(line > 0, lines[0, :, WIDTH : 2 * WIDTH].astype(f32), 0.0)
    grad = jnp.where(line < HALF - 1, lines[HALF - 1, :, WIDTH:].astype(f32), 0.0)
    for i in range(1, HALF - 1):
        state = jnp.where(i < line, advance(lines[i], state), state)
        back = HALF - 1 - i
        grad = jnp.where(back > line, retreat(lines[back], grad), grad)
    for i in range(HALF):
        found[i, :, :WIDTH] = state.astype(bf16)
        back = HALF - 1 - i
        found[back, :, WIDTH:] = grad.astype(bf16)
        if i < HALF - 1:
            state = advance(chips[i], state)
            grad = retreat(chips[back], grad)
    for shift, out in enumerate((o0, o1, o2, o3)):
        out[...] = found[lax.rem(spot + shift, HALF)]


def down_kernel(a_ref, b_ref, c_ref, d_ref, keep_ref, got_ref, gkeep_ref, ggot_ref, own_ref, send_ref, slots):
    core, spot, unused = here()
    gather_slots(slots, (a_ref, b_ref, c_ref, d_ref), spot)
    for slot in range(HALF):
        state = slots[slot, :, :WIDTH]
        grad = slots[slot, :, WIDTH:]
        first = jnp.where(core == 0, keep_ref[slot].astype(f32), got_ref[slot].astype(f32))
        second = jnp.where(core == 0, got_ref[slot, :, :WIDTH].astype(f32), keep_ref[slot, :, :WIDTH].astype(f32))
        gsecond = jnp.where(core == 0, ggot_ref[slot].astype(f32), gkeep_ref[slot].astype(f32))
        middle = state.astype(f32) - nn(first[:, :WIDTH].astype(bf16), state) + first[:, WIDTH:]
        gmiddle = grad.astype(f32) - tn(second.astype(bf16), grad) + gsecond
        early = jnp.concatenate([state.astype(f32), gmiddle], axis=1)
        late = jnp.concatenate([middle, grad.astype(f32)], axis=1)
        own_ref[slot] = jnp.where(core == 0, early, late).astype(bf16)
        send_ref[slot] = jnp.where(core == 0, late, early).astype(bf16)


def grads_kernel(
    k_ref, q_ref, b_ref, do_ref, yh_ref, yl_ref, z_ref, ph_ref, pl_ref, u_ref, own_ref, got_ref,
    dq_ref, dk_ref, dv_ref, db_ref,
):
    step = pl.program_id(0)
    core = here()[0]
    heads = range(GRADS_HEADS)
    parts = range(2)
    both = [(h, p) for h in heads for p in parts]
    tokens = q_ref.shape[0]
    half = tokens // 2
    rows = 2 * half
    diagonal = eye_mask(rows)
    before = order((rows, rows), 1) < order((rows, rows), 0)
    seen = order((half, rows), 1) < 2 * (iota((half, rows), 0) + 1)
    seen_t = order((rows, half), 0) < 2 * (iota((rows, half), 1) + 1)
    state, after = [], []
    for h in heads:
        head = step * GRADS_HEADS + h
        slot = lax.rem(head, HALF)
        mine = head // HALF == core
        ends = jnp.where(mine, own_ref[slot].astype(f32), got_ref[slot].astype(f32)).astype(bf16)
        state.append(ends[:, :WIDTH])
        after.append(ends[:, WIDTH:])
    keys = {(h, p): pick(k_ref, h, p) for h, p in both}
    rate = {(h, p): column(rate_row(b_ref, h, p), diagonal) for h, p in both}
    norm = {c: inverse_norms(keys[c]) for c in both}
    query = [q_ref[:, h * WIDTH : (h + 1) * WIDTH] for h in heads]

    errors, back = {}, {}
    for h, p in both:
        errors[h, p] = nn(yh_ref[h, p], state[h]) + nn(yl_ref[h, p], state[h]) - z_ref[h, p]
        back[h, p] = -u_ref[h, p] - nn(ph_ref[h, p], after[h]) - nn(pl_ref[h, p], after[h])
    weighted = {c: errors[c] * rate[c] for c in both}
    scaled = {c: back[c] * rate[c] for c in both}
    d_rate = {c: jnp.sum(errors[c] * back[c], axis=1, keepdims=True) for c in both}
    d_rate = {c: jnp.sum(jnp.where(diagonal, d_rate[c], 0.0), axis=0, keepdims=True) for c in both}
    for h, p in both:
        db_ref[h, 0:1, p * half : (p + 1) * half] = d_rate[h, p][:, :half]
        db_ref[h, 1:2, p * half : (p + 1) * half] = d_rate[h, p][:, half:]
        put(dv_ref, h, p, (-scaled[h, p]).astype(bf16))
    ws = {c: split(weighted[c]) for c in both}
    fs = {c: split(scaled[c]) for c in both}
    wn = [jnp.concatenate([(weighted[h, p] * norm[h, p]).astype(bf16) for p in parts], axis=0) for h in heads]
    fn = [jnp.concatenate([(scaled[h, p] * norm[h, p]).astype(bf16) for p in parts], axis=0) for h in heads]
    all_keys = [jnp.concatenate([keys[h, p] for p in parts], axis=0) for h in heads]

    score = [nt(do_ref[h], wn[h]) for h in heads]
    score_t = {(h, p): nt(ws[h, p][0], do_ref[h] if p == 0 else do_ref[h, half:]) for h, p in both}
    lower, upper = {}, {}
    for h, p in both:
        first = jnp.concatenate(ws[h, p], axis=1)
        second = jnp.concatenate(fs[h, p], axis=1)
        wn2 = jnp.concatenate([wn[h], wn[h]], axis=1)
        fn2 = jnp.concatenate([fn[h], fn[h]], axis=1)
        upper[h, p] = nt(first, fn2 if p == 0 else fn2[rows:])
        lower[h, p] = nt(second, wn2[:rows] if p == 0 else wn2)
    pairs, reads = {}, {}
    for h, p in both:
        if p == 0:
            own = jnp.where(before, lower[h, p], jnp.where(diagonal, 0.0, upper[h, p][:, :rows]))
            pairs[h, p] = jnp.concatenate([own, upper[h, p][:, rows:]], axis=1).astype(bf16)
            masked = jnp.concatenate(
                [jnp.where(seen_t, score_t[h, p][:, :half], 0.0), score_t[h, p][:, half:]], axis=1
            )
            reads[h, p] = nn(masked.astype(bf16), query[h])
        else:
            own = jnp.where(before, lower[h, p][:, rows:], jnp.where(diagonal, 0.0, upper[h, p]))
            pairs[h, p] = jnp.concatenate([lower[h, p][:, :rows], own], axis=1).astype(bf16)
            reads[h, p] = nn(jnp.where(seen_t, score_t[h, p], 0.0).astype(bf16), query[h][half:])
    for h in heads:
        masked = jnp.concatenate([
            jnp.concatenate([jnp.where(seen, score[h][:half, :rows], 0.0), jnp.zeros((half, rows), f32)], axis=1),
            jnp.concatenate([score[h][half:, :rows], jnp.where(seen, score[h][half:, rows:], 0.0)], axis=1),
        ], axis=0).astype(bf16)
        dq = nt(do_ref[h], state[h]) - nn(masked, all_keys[h])
        dq_ref[:, h * WIDTH : (h + 1) * WIDTH] = (dq * SCALE).astype(bf16)
    dk = {
        (h, p): nt(fs[h, p][0], state[h]) - reads[h, p] * SCALE - nt(ws[h, p][0], after[h]) - nn(pairs[h, p], all_keys[h])
        for h, p in both
    }
    units = {c: keys[c].astype(f32) * norm[c] for c in both}
    along = {c: jnp.sum(units[c] * dk[c], axis=1, keepdims=True) for c in both}
    for h, p in both:
        put(dk_ref, h, p, (norm[h, p] * (dk[h, p] - units[h, p] * along[h, p])).astype(bf16))


def whole(shape):
    return pl.BlockSpec(shape, lambda *unused: (0,) * len(shape))


def run(kernel, name, args, in_specs, outs, out_specs, grid=(1,), scratch=(), cost=None, vmem=16):
    return pl.pallas_call(
        kernel,
        name=name,
        grid=grid,
        in_specs=in_specs,
        out_specs=out_specs,
        scratch_shapes=list(scratch),
        out_shape=[jax.ShapeDtypeStruct(shape, dtype) for shape, dtype in outs],
        compiler_params=pltpu.CompilerParams(vmem_limit_bytes=vmem * 2**20),
        cost_estimate=cost,
    )(*args)


def small(kernel, name, args, outs, scratch=()):
    return run(
        kernel, name, args,
        [whole(a.shape) for a in args],
        outs,
        [whole(shape) for shape, unused in outs],
        scratch=scratch,
    )


def shards(queries, key_input, value_input, beta_rates, out_grad, out_weight):
    tokens = queries.shape[0]
    heads = queries.shape[1] // WIDTH
    rows = 2 * tokens
    model = out_weight.shape[1]
    near_keys, near_queries, near_rates = key_input, queries, beta_rates
    key_input, value_input, queries, out_weight, beta_rates = (
        pltpu.with_memory_space_constraint(a, pltpu.HBM)
        for a in (key_input, value_input, queries, out_weight, beta_rates)
    )

    def move(value, target):
        return lax.ppermute(value, "ctx", [(i, target(i)) for i in range(32)])

    def other_core(i):
        return i ^ 1

    def along_x(by):
        return lambda i: (i // 8) * 8 + ((i // 2 + by) % HALF) * 2 + i % 2

    def along_y(by):
        return lambda i: (i + 8 * by) % 32

    def kv_spec(count):
        return pl.BlockSpec((2, tokens, count * WIDTH), lambda s: (0, 0, s))

    def q_spec(count):
        return pl.BlockSpec((tokens, count * WIDTH), lambda s: (0, s))

    def b_spec(count):
        return pl.BlockSpec((count, 2, tokens), lambda s: (s, 0, 0))

    def by_step(count, *shape):
        return pl.BlockSpec((count,) + shape, lambda s: (s,) + (0,) * len(shape))

    gathered = [out_grad] + [
        lax.ppermute(out_grad, "head", [(i, (i + by) % HALF) for i in range(HALF)]) for by in (1, 3, 2)
    ]
    gathered = [gathered[0], gathered[1], gathered[3], gathered[2]]
    tile = (2, tokens, tokens)
    send, keep, nh, nl, yh, yl, z, sh, sl, rh, rl, ph, plow, near = run(
        maps_kernel, "maps", (key_input, value_input, queries, beta_rates, out_weight),
        [kv_spec(MAPS_HEADS), kv_spec(MAPS_HEADS), q_spec(MAPS_HEADS), b_spec(MAPS_HEADS), pl.BlockSpec(memory_space=pl.ANY)],
        [((HALF, WIDTH, 2 * WIDTH), bf16)] * 2 + [((heads,) + tile, bf16)] * 4 + [((heads,) + tile, f32)]
        + [((heads,) + tile, bf16)] * 2 + [((heads, tokens, WIDTH), bf16)] * 2 + [((heads,) + tile, bf16)] * 2 + [(out_weight.shape, bf16)],
        [whole((HALF, WIDTH, 2 * WIDTH))] * 2 + [by_step(MAPS_HEADS, *tile)] * 7
        + [by_step(MAPS_HEADS, tokens, WIDTH)] * 2 + [by_step(MAPS_HEADS, *tile)] * 2 + [pl.BlockSpec(memory_space=pltpu.VMEM)],
        grid=(heads // MAPS_HEADS,),
        scratch=[pltpu.SemaphoreType.DMA],
        vmem=30,
        cost=pl.CostEstimate(flops=14_000_000_000, transcendentals=0, bytes_accessed=8_000_000),
    )
    got = move(send, other_core)
    gsend, gkeep, grad = run(
        local_grad_kernel, "local_grad", (*gathered, near, rh, rl),
        [
            *[whole(out_grad.shape)] * HALF,
            pl.BlockSpec(memory_space=pltpu.VMEM),
            *[by_step(LOCAL_HEADS, tokens, WIDTH)] * 2,
        ],
        [((HALF, WIDTH, WIDTH), bf16)] * 2 + [((heads, tokens, WIDTH), bf16)],
        [whole((HALF, WIDTH, WIDTH))] * 2 + [by_step(LOCAL_HEADS, tokens, WIDTH)],
        grid=(heads // LOCAL_HEADS,),
        scratch=[pltpu.VMEM((tokens, model), bf16)],
        vmem=24,
        cost=pl.CostEstimate(flops=2_000_000_000, transcendentals=0, bytes_accessed=10_000_000),
    )
    ggot = move(gsend, other_core)
    map_shape = ((WIDTH, 3 * WIDTH), bf16)
    chip = small(pair_kernel, "pair", (keep, got, gkeep, ggot), [map_shape] * HALF)
    chip = list(chip)
    chip[0], grad = lax.optimization_barrier((chip[0], grad))
    (reached,) = run(
        prep_kernel, "prep", (near_keys, near_rates, grad, nh, nl, sh, sl),
        [
            kv_spec(PREP_HEADS), b_spec(PREP_HEADS), by_step(PREP_HEADS, tokens, WIDTH),
            *[by_step(PREP_HEADS, *tile)] * 4,
        ],
        [((heads,) + tile, f32)],
        [by_step(PREP_HEADS, *tile)],
        grid=(heads // PREP_HEADS,),
        vmem=24,
        cost=pl.CostEstimate(flops=4_000_000_000, transcendentals=0, bytes_accessed=6_000_000),
    )
    chip = [chip[0]] + [move(chip[by], along_x(by)) for by in range(1, HALF)]
    chip[0], reached = lax.optimization_barrier((chip[0], reached))
    slots = pltpu.VMEM((HALF, WIDTH, 3 * WIDTH), bf16)
    ends_shape = ((WIDTH, 2 * WIDTH), bf16)
    line = small(row_kernel, "line", chip, [ends_shape] * (HALF - 1), [slots])
    lines = [move(line[by - 1], along_y(by)) for by in range(1, HALF)]
    ends_slots = pltpu.VMEM((HALF, WIDTH, 2 * WIDTH), bf16)
    ends = small(expand_kernel, "expand", chip + lines, [ends_shape] * HALF, [slots, ends_slots, ends_slots])
    ends = [ends[0]] + [move(ends[by], along_x(by)) for by in range(1, HALF)]
    own, passed = small(
        down_kernel, "down", ends + [keep, got, gkeep, ggot],
        [((HALF, WIDTH, 2 * WIDTH), bf16)] * 2, [ends_slots],
    )
    taken = move(passed, other_core)
    return tuple(run(
        grads_kernel, "grads",
        (near_keys, near_queries, near_rates, grad, yh, yl, z, ph, plow, reached, own, taken),
        [
            kv_spec(GRADS_HEADS), q_spec(GRADS_HEADS), b_spec(GRADS_HEADS), by_step(GRADS_HEADS, tokens, WIDTH),
            *[by_step(GRADS_HEADS, *tile)] * 6,
            whole((HALF, WIDTH, 2 * WIDTH)), whole((HALF, WIDTH, 2 * WIDTH)),
        ],
        [
            (queries.shape, bf16), (key_input.shape, bf16), (value_input.shape, bf16), (beta_rates.shape, f32),
        ],
        [q_spec(GRADS_HEADS), kv_spec(GRADS_HEADS), kv_spec(GRADS_HEADS), b_spec(GRADS_HEADS)],
        grid=(heads // GRADS_HEADS,),
        vmem=24,
        cost=pl.CostEstimate(flops=8_000_000_000, transcendentals=0, bytes_accessed=14_000_000),
    ))


def solution(mesh):
    placed = (
        P("ctx", "head"),
        P(None, "ctx", "head"),
        P(None, "ctx", "head"),
        P("head", None, "ctx"),
        P(("ctx", "head"), None),
        P("head", None),
    )
    return jax.shard_map(
        shards,
        mesh=mesh,
        in_specs=placed,
        out_specs=(
            P("ctx", "head"),
            P(None, "ctx", "head"),
            P(None, "ctx", "head"),
            P("head", None, "ctx"),
        ),
        check_vma=False,
    )
```
